32 devices in a mesh: fsdp: 8 (over z, x), seq: 4 (over y, core).
Axes of the slice: x: 2, y: 2, z: 4, core: 2. Of those that a mesh axis runs over, the one named last changes fastest.
Arguments:
- context: bfloat16 [16, 512, 2560], P('fsdp', 'seq'), may hold values from -6 to 6
- residual: bfloat16 [16, 512, 2560], P('fsdp', 'seq'), may hold values from -6 to 6
- target_rows: bfloat16 [16, 512, 2560], P('fsdp', 'seq'), may hold values from -0.00390625 to 0.00390625
- log_norm: float32 [16, 512], P('fsdp', 'seq'), may hold values from -0.15 to 0.15
- norm_gain: float32 [2560], replicated, may hold values from 0.1 to 1.9
- out_proj: bfloat16 [2560, 2560], P('fsdp'), may hold values from -0.125 to 0.125
- old_logprob: float32 [16, 512], P('fsdp', 'seq'), may hold values from -0.15 to 0.15
- lengths: int32 [16, 4], P('fsdp', 'seq'), may hold values from 112 to 128
- rewards: float32 [16, 4], P('fsdp', 'seq'), may hold values from -5 to 5
- prompt_ids: int32 [16, 4], P('fsdp', 'seq'), may hold values from 0 to 3, as said below
- placement: int32 [16, 4], P('fsdp', 'seq'), may hold values from 0 to 15, as said below
Outputs:
- grad_context: bfloat16 [16, 512, 2560], P('fsdp', 'seq')
- grad_weight: float32 [2560, 2560], P('fsdp')
- loss: float32 [], replicated
The draws below stay inside these ranges and needn't reach their ends.
Inputs may be any that keep to these rules, and one draw needn't show every extreme that they name: `prompt_ids`: every prompt id names exactly 16 rows. Sampler row (a, s) goes to learner row (placement[a, s], s) and keeps a mod 2; the 2 rows of one device go to 2 different fsdp indices; every learner row receives exactly one row; in every column one of the 2 rows of each device goes 8 / 2 fsdp indices onward and another goes 1 index onward, counted round.
All inputs are finite; a program needn't handle non-finite values.
Results may differ from the reference program's by a relative error of at most 0.014.
Values may be sent and summed in bfloat16 or wider, within the bound.
A program may use at most 128 MiB of HBM per device.

```python
import math
import jax
import jax.numpy as jnp
from jax import lax

DW = 2560
AW = 2560
RS = 2
LMAX = 128
GS = 16
FSDP_WAYS = 8
SEQ_WAYS = 4
FROWS = 16
POSITIONS = 512
ROWS_ALL = 64
PROMPTS = 4
ALL_TOKENS = 8192


def draw_prompt_ids(key, part):
    order = jax.random.permutation(key, ROWS_ALL)
    return (order // GS).astype(jnp.int32).reshape(FROWS, SEQ_WAYS)


def pick_shifts(subkey):
    first_key, second_key = jax.random.split(subkey)
    halfway = FSDP_WAYS // 2
    others = jax.random.permutation(first_key, FSDP_WAYS - 2).astype(jnp.int32)
    others = jnp.where(others >= 1, others + 1, others)
    others = jnp.where(others >= halfway, others + 1, others)
    chosen = jnp.concatenate([jnp.full((1,), halfway, jnp.int32), jnp.ones((1,), jnp.int32), others[:RS - 2]])
    return chosen[jax.random.permutation(second_key, RS)]


def draw_placement(key, part):
    subkeys = jax.random.split(jax.random.fold_in(key, 7), SEQ_WAYS)
    shifts = jax.vmap(pick_shifts)(subkeys)
    row_index = jnp.arange(FROWS, dtype=jnp.int32)
    owner = row_index // RS
    within = row_index % RS
    moved = shifts.T[within]
    target = (owner[:, None] + moved) % FSDP_WAYS
    return (target * RS + within[:, None]).astype(jnp.int32)


def place_ends(drawn, key, low, largest):
    place = [jax.random.randint(jax.random.fold_in(key, axis), (), 0, length) for axis, length in enumerate(drawn.shape)]
    longest = drawn.shape.index(max(drawn.shape))
    next_to = place[:longest] + [(place[longest] + 1) % drawn.shape[longest]] + place[longest + 1:]
    return drawn.at[tuple(place)].set(low).at[tuple(next_to)].set(largest)


def block_scale(rng, dims, cuts, least, high):
    gain, own = 1.0, jax.random.fold_in(rng, 6)
    for position, shards_of in cuts:
        heights = jnp.exp(jax.random.uniform(jax.random.fold_in(own, position), (shards_of,), jnp.float32, least / len(cuts), high / len(cuts)))
        gain = gain * jnp.repeat(heights, dims[position] // shards_of).reshape([-1 if axis == position else 1 for axis in range(len(dims))])
    return gain


def normal_values(own_key, extent, spread, bound, shards=(), kind=jnp.bfloat16):
    entries = jax.random.normal(own_key, extent, jnp.float32) * spread
    if len(shards) > 0:
        entries = block_scale(own_key, extent, shards, -0.22, 0.18) * entries
    return jnp.clip(entries, min=-bound, max=bound).astype(kind)


def setup_inputs(seed: int = 0) -> dict:
    splits = jax.random.split(jax.random.key(seed), 12)
    context = normal_values(splits[0], (FROWS, POSITIONS, AW), 1.0, 6.0, ((0, 8), (1, 4)))
    residual = normal_values(splits[1], (FROWS, POSITIONS, DW), 1.0, 6.0, ((0, 8), (1, 4)))
    target_rows = normal_values(splits[2], (FROWS, POSITIONS, DW), (1024 * DW) ** -0.5, 0.00390625, ((0, 8), (1, 4)))
    log_norm = normal_values(splits[3], (FROWS, POSITIONS), 0.05, 0.15, ((0, 8), (1, 4)), jnp.float32)
    norm_gain = jnp.clip(1.0 + 0.18 * jax.random.normal(splits[4], (DW,), jnp.float32), 0.1, 1.9)
    out_proj = normal_values(splits[5], (AW, DW), AW ** -0.5, 0.125, ((0, 8),))
    old_logprob = normal_values(splits[6], (FROWS, POSITIONS), 0.05, 0.15, ((0, 8), (1, 4)), jnp.float32)
    lengths = place_ends(jax.random.randint(splits[7], (FROWS, SEQ_WAYS), LMAX - LMAX // 8, LMAX + 1), jax.random.fold_in(splits[7], 1), LMAX - LMAX // 8, LMAX).astype(jnp.int32)
    rewards = normal_values(splits[8], (FROWS, SEQ_WAYS), 1.0, 5.0, ((0, 8), (1, 4)), jnp.float32)
    prompt_ids = draw_prompt_ids(jax.random.fold_in(splits[11], 71), 0)
    placement = draw_placement(jax.random.fold_in(splits[11], 71), 0)
    return dict(context=context, residual=residual, target_rows=target_rows, log_norm=log_norm, norm_gain=norm_gain, out_proj=out_proj, old_logprob=old_logprob, lengths=lengths, rewards=rewards, prompt_ids=prompt_ids, placement=placement)


def reference(context, residual, target_rows, log_norm, norm_gain, out_proj, old_logprob, lengths, rewards, prompt_ids, placement):
    reward_flat = rewards.reshape(-1)
    prompt_flat = prompt_ids.reshape(-1)
    onehot = (prompt_flat[:, None] == jnp.arange(PROMPTS, dtype=jnp.int32)[None, :]).astype(jnp.float32)
    group_sum = lax.optimization_barrier(jnp.sum(onehot * reward_flat[:, None], axis=0))
    group_sq = lax.optimization_barrier(jnp.sum(onehot * (reward_flat * reward_flat)[:, None], axis=0))
    count = jnp.sum(lengths.astype(jnp.float32))
    group_mean = group_sum / GS
    group_var = group_sq / GS - group_mean * group_mean
    row_mean = lax.optimization_barrier(jnp.sum(onehot * group_mean[None, :], axis=1))
    row_var = lax.optimization_barrier(jnp.sum(onehot * group_var[None, :], axis=1))
    advantage = ((reward_flat - row_mean) / jnp.sqrt(row_var + 0.25)).reshape(FROWS, SEQ_WAYS)
    column = jnp.broadcast_to(jnp.arange(SEQ_WAYS, dtype=jnp.int32)[None, :], (FROWS, SEQ_WAYS))
    learn_adv = jnp.zeros((FROWS, SEQ_WAYS), jnp.float32).at[placement, column].set(advantage)
    learn_len = jnp.zeros((FROWS, SEQ_WAYS), jnp.int32).at[placement, column].set(lengths)
    old_blocks = old_logprob.reshape(FROWS, SEQ_WAYS, LMAX)
    learn_old = jnp.zeros((FROWS, SEQ_WAYS, LMAX), jnp.float32).at[placement, column].set(old_blocks)
    offsets = jnp.arange(LMAX, dtype=jnp.int32)
    valid = (offsets[None, None, :] < learn_len[:, :, None]).astype(jnp.float32).reshape(-1)
    token_adv = jnp.broadcast_to(learn_adv[:, :, None], (FROWS, SEQ_WAYS, LMAX)).reshape(-1)
    context_flat = context.reshape(-1, AW)
    hidden = residual.reshape(-1, DW).astype(jnp.float32) + jnp.dot(context_flat, out_proj, preferred_element_type=jnp.float32)
    rinv = lax.rsqrt(lax.optimization_barrier(jnp.mean(hidden * hidden, axis=1)) + 1e-06)
    vecs = norm_gain[None, :] * target_rows.reshape(-1, DW).astype(jnp.float32)
    hv_sum = lax.optimization_barrier(jnp.sum(hidden * vecs, axis=1))
    score = hv_sum * rinv
    ratio = jnp.exp(score - log_norm.reshape(-1) - learn_old.reshape(-1))
    plain = ratio * token_adv
    clipped = jnp.clip(ratio, 0.8, 1.2) * token_adv
    objective = jnp.minimum(plain, clipped)
    loss = jnp.sum(valid * -objective) / count
    dscore = -valid * jnp.where(plain <= clipped, plain, 0.0) / count
    dhid = (dscore * rinv)[:, None] * (vecs - hidden * (rinv * rinv * hv_sum / DW)[:, None])
    grad_hidden = (dhid * (32.0 * ALL_TOKENS * math.sqrt(DW))).astype(jnp.bfloat16)
    grad_context = jnp.dot(grad_hidden, out_proj.T, preferred_element_type=jnp.float32).astype(jnp.bfloat16)
    grad_context = grad_context.reshape(FROWS, POSITIONS, AW)
    ctx_dev = context.reshape(FSDP_WAYS, RS, SEQ_WAYS, LMAX, AW).transpose(0, 2, 1, 3, 4).reshape(FSDP_WAYS * SEQ_WAYS, RS * LMAX, AW)
    grad_dev = grad_hidden.reshape(FSDP_WAYS, RS, SEQ_WAYS, LMAX, DW).transpose(0, 2, 1, 3, 4).reshape(FSDP_WAYS * SEQ_WAYS, RS * LMAX, DW)

    def add_device(total, pieces):
        term = lax.dot_general(pieces[0], pieces[1], (((0,), (0,)), ((), ())), preferred_element_type=jnp.float32)
        term = lax.optimization_barrier(term.astype(jnp.bfloat16))
        return (total + term.astype(jnp.float32), None)
    total, unused = lax.scan(add_device, jnp.zeros((AW, DW), jnp.float32), (ctx_dev, grad_dev))
    grad_weight = total * (1.0 / math.sqrt(ALL_TOKENS))
    return (grad_context, grad_weight, loss)
```

```python
import functools
import math

import jax
import jax.numpy as jnp
from jax import lax
from jax.experimental import pallas as pl
from jax.experimental.pallas import tpu as pltpu
from jax.sharding import PartitionSpec as P

GS = 16
FO = 4
Q = 4
MESH = pl.DeviceIdType.MESH
F32 = jnp.float32
BF16 = jnp.bfloat16
NT = (((1,), (1,)), ((), ()))


def kernel(
    dims,
    ctx_in,
    res_in,
    tgt_in,
    lognorm,
    gain1,
    w_in,
    old,
    rewards,
    prompt_ids,
    lengths,
    placement,
    gctx_out,
    gw_out,
    loss_out,
    w,
    ctx,
    ctxt,
    res,
    tgt,
    hid,
    gh,
    sm,
    rb,
    dws,
    irecv,
    part,
    obuf,
    orecv,
    fsend,
    frecv,
    acc,
    gdiag,
    gcore,
    gfar,
    rdiag,
    rcore,
    rfar,
    pk,
    ls,
    gain,
    loc,
    ag_o,
    ag_i,
    tok,
    gx,
    sx,
    rs_i,
    rs_o,
    fin,
    pk1,
    pk2,
    pk3,
    ls2,
    ls3,
):
    fsdp_ways, seq_ways, nrows, lmax, dw, aw = dims
    fi = fsdp_ways // FO
    so_ways = seq_ways // Q
    tokens = nrows * lmax
    blk = aw // fsdp_ways
    cq = dw // Q
    prompts = nrows * fsdp_ways * seq_ways // GS
    prows = max(8, prompts)
    all_tokens = tokens * fsdp_ways * seq_ways
    f = lax.axis_index("fsdp")
    s = lax.axis_index("seq")
    o = f // fi
    i = lax.rem(f, fi)
    so = s // Q
    q = lax.rem(s, Q)
    c = lax.rem(q, 2)

    def outer_dev(k, m=0):
        return (lax.rem(o + k, FO) * fi + i, lax.rem(so + m, so_ways) * Q + q)

    def inner_dev(j):
        return (o * fi + lax.rem(i + j, fi), s)

    def group_dev(k):
        return (f, so * Q + lax.rem(q + k, Q))

    q_core = q + 1 - 2 * c
    q_far = lax.rem(q + 2, Q)
    q_diag = lax.rem(q_core + 2, Q)
    core_dev = (f, so * Q + q_core)
    far_dev = (f, so * Q + q_far)
    diag_dev = (f, so * Q + q_diag)
    outer = [(m, k) for k in range(FO) for m in range(so_ways) if (m, k) != (0, 0)]
    ring = (1, 3, 2)

    def rows_of(owner):
        return pl.ds(pl.multiple_of(owner * blk, blk), blk)

    def cols_of(quarter):
        return pl.ds(pl.multiple_of(quarter * cq, 128), cq)

    def toks_of(quarter):
        return pl.ds(pl.multiple_of(quarter * tokens, 128), tokens)

    def local(src, dst, index):
        copy = pltpu.make_async_copy(src, dst, loc.at[index])
        copy.start()
        return copy

    own_w = local(w_in.at[:, cols_of(q)], w.at[rows_of(f), :], 0)
    own_ctx = local(ctx_in, ctx.at[q], 1)
    own_res = local(res_in.at[:, cols_of(q)], res.at[q], 2)
    own_tgt = local(tgt_in.at[:, cols_of(q)], tgt.at[q], 3)

    barrier = pltpu.get_barrier_semaphore()
    peers = [outer_dev(k, m) for m, k in outer]
    peers += [inner_dev(j) for j in range(1, fi)]
    peers += [group_dev(k) for k in range(1, Q)]
    for peer in peers:
        pl.semaphore_signal(barrier, inc=1, device_id=peer, device_id_type=MESH)

    at_home = (o, so, i, q)
    pk[at_home] = jnp.zeros((16, 128), F32)
    pk[at_home + (pl.ds(0, nrows), slice(None))] = old[...]
    for n, field in enumerate((rewards, prompt_ids, lengths, placement)):
        for r in range(nrows):
            pk[at_home + (pl.ds((n + 1) * nrows + r, 1), slice(None))] = jnp.broadcast_to(
                field[:, r : r + 1].astype(F32), (1, 128)
            )
    pk[at_home + (pl.ds(5 * nrows, nrows), slice(None))] = lognorm[...]
    gain[...] = gain1[...].reshape(1, dw)

    pl.semaphore_wait(barrier, len(peers))

    sent = []

    def send(src, dst, sems, index, dev):
        copy = pltpu.make_async_remote_copy(
            src_ref=src,
            dst_ref=dst,
            send_sem=sems.at[(0,) + index],
            recv_sem=sems.at[(1,) + index],
            device_id=dev,
            device_id_type=MESH,
        )
        copy.start()
        sent.append(copy)

    def arrive(dst, sems, index, dev):
        pltpu.make_async_remote_copy(
            src_ref=dst,
            dst_ref=dst,
            send_sem=sems.at[(0,) + index],
            recv_sem=sems.at[(1,) + index],
            device_id=dev,
            device_id_type=MESH,
        ).wait_recv()

    def block(owner):
        return w.at[rows_of(owner), :]

    for k in range(1, Q):
        mine = pk.at[o, so, i, q]
        send(mine, mine, pk1, (k,), group_dev(k))
    for j in range(1, fi):
        send(w_in.at[:, cols_of(q)], block(f), ag_i, (0, j), inner_dev(j))
    for k in ring:
        send(w_in.at[:, cols_of(q)], block(f), ag_o, (k,), outer_dev(k))
    send(ctx_in, ctx.at[q], tok, (0,), far_dev)
    send(ctx_in, ctx.at[q], tok, (1,), core_dev)
    send(res_in.at[:, cols_of(q_core)], res.at[q], tok, (3,), core_dev)
    send(tgt_in.at[:, cols_of(q_core)], tgt.at[q], tok, (4,), core_dev)
    send(res_in.at[:, cols_of(q_far)], res.at[q], tok, (5,), far_dev)
    send(tgt_in.at[:, cols_of(q_far)], tgt.at[q], tok, (6,), far_dev)
    send(res_in.at[:, cols_of(q_diag)], res.at[q], tok, (7,), diag_dev)
    send(tgt_in.at[:, cols_of(q_diag)], tgt.at[q], tok, (8,), diag_dev)

    def turn(a):
        @pl.loop(0, aw // 256)
        def _(t):
            span = pl.ds(pl.multiple_of(t * 256, 256), 256)
            ctxt[span, toks_of(a)] = ctx[a, :, span].T

    for k in range(1, Q):
        there = pk.at[o, so, i, lax.rem(q + Q - k, Q)]
        arrive(there, pk1, (k,), group_dev(k))
    for j in range(1, fi):
        mine = pk.at[o, so, i]
        send(mine, mine, pk2, (j,), inner_dev(j))
    own_ctx.wait()
    turn(q)
    arrive(ctx.at[q_core], tok, (1,), core_dev)
    turn(q_core)

    for j in range(1, fi):
        owner = o * fi + lax.rem(i + fi - j, fi)
        arrive(block(owner), ag_i, (0, j), inner_dev(j))
    for j in range(1, fi):
        there = pk.at[o, so, lax.rem(i + fi - j, fi)]
        arrive(there, pk2, (j,), inner_dev(j))
    for m, k in outer:
        mine = pk.at[o, so]
        send(mine, mine, pk3, (m, k), outer_dev(k, m))

    def pass_on(k):
        here = block(lax.rem(o + FO - k, FO) * fi + i)
        arrive(here, ag_o, (k,), outer_dev(k))
        for j in range(1, fi):
            send(here, here, ag_i, (k, j), inner_dev(j))

    pass_on(1)
    pass_on(3)
    arrive(ctx.at[q_far], tok, (0,), far_dev)
    send(ctx.at[q_far], ctx.at[q_far], tok, (2,), core_dev)
    pass_on(2)
    turn(q_far)
    arrive(ctx.at[q_diag], tok, (2,), core_dev)
    turn(q_diag)

    for m, k in outer:
        there = pk.at[lax.rem(o + FO - k, FO), lax.rem(so + so_ways - m, so_ways)]
        arrive(there, pk3, (m, k), outer_dev(k, m))

    prompt_row = lax.broadcasted_iota(jnp.int32, (prows, 128), 0).astype(F32)
    zero_p = jnp.zeros((prows, 128), F32)
    zero_r = jnp.zeros((1, 128), F32)

    def over_devices(fa, carry):
        for sa in range(seq_ways):
            at = (fa // fi, sa // Q, lax.rem(fa, fi), sa % Q)
            for r in range(nrows):
                gsum, gsq, count = carry
                reward = pk[at + (pl.ds(nrows + r, 1), slice(None))]
                prompt = pk[at + (pl.ds(2 * nrows + r, 1), slice(None))]
                length = pk[at + (pl.ds(3 * nrows + r, 1), slice(None))]
                hot = prompt == prompt_row
                gsum = gsum + jnp.where(hot, reward, 0.0)
                gsq = gsq + jnp.where(hot, reward * reward, 0.0)
                carry = (gsum, gsq, count + length)
        return carry

    gsum, gsq, count = lax.fori_loop(0, fsdp_ways, over_devices, (zero_p, zero_p, zero_r))
    gmean = gsum / GS
    gvar = gsq / GS - gmean * gmean
    offset = lax.broadcasted_iota(jnp.int32, (1, lmax), 1).astype(F32)
    count1 = count[:, 0:1]

    for a in range(Q):

        def over_column(fa, carry, a=a):
            at = (fa // fi, so, lax.rem(fa, fi), a)
            for r in range(nrows):
                past = pk[at + (pl.ds(r, 1), slice(None))]
                reward = pk[at + (pl.ds(nrows + r, 1), slice(None))]
                prompt = pk[at + (pl.ds(2 * nrows + r, 1), slice(None))]
                length = pk[at + (pl.ds(3 * nrows + r, 1), slice(None))]
                dest = pk[at + (pl.ds(4 * nrows + r, 1), slice(None))]
                hot = prompt == prompt_row
                mean = jnp.sum(jnp.where(hot, gmean, 0.0), axis=0, keepdims=True)
                var = jnp.sum(jnp.where(hot, gvar, 0.0), axis=0, keepdims=True)
                adv = (reward - mean) / jnp.sqrt(var + 0.25)
                fresh = []
                for j in range(nrows):
                    chosen = dest == (f * nrows + j).astype(F32)
                    l_old, l_adv, l_len = carry[3 * j : 3 * j + 3]
                    fresh += [
                        l_old + jnp.where(chosen, past, 0.0),
                        l_adv + jnp.where(chosen, adv, 0.0),
                        l_len + jnp.where(chosen, length, 0.0),
                    ]
                carry = tuple(fresh)
            return carry

        learned = lax.fori_loop(0, fsdp_ways, over_column, (zero_r,) * (3 * nrows))
        for j in range(nrows):
            l_old, l_adv, l_len = learned[3 * j : 3 * j + 3]
            at = pl.ds(a * tokens + j * lmax, lmax)
            norm = pk[o, so, i, a, pl.ds(5 * nrows + j, 1), :]
            rb[0:1, at] = norm + l_old
            rb[1:2, at] = l_adv
            rb[2:3, at] = (offset < l_len).astype(F32)

    own_w.wait()
    own_res.wait()
    own_tgt.wait()
    for k in ring:
        for j in range(1, fi):
            owner = lax.rem(o + FO - k, FO) * fi + lax.rem(i + fi - j, fi)
            arrive(block(owner), ag_i, (k, j), inner_dev(j))

    @pl.loop(0, Q)
    def _(a):
        hid[a] = jnp.dot(ctx[a], w[...], preferred_element_type=F32)

    lane = lax.broadcasted_iota(jnp.int32, (tokens, 128), 1)

    def sums(a):
        h = hid[a] + res[a].astype(F32)
        hid[a] = h
        v = gain[:, cols_of(q)] * tgt[a].astype(F32)
        ssq = jnp.sum(h * h, axis=1, keepdims=True)
        shv = jnp.sum(h * v, axis=1, keepdims=True)
        both = jnp.where(lane == 0, ssq, jnp.where(lane == 1, shv, 0.0))
        sm[q, :, toks_of(a)] = both.T[0:8, :]

    sums(q)
    arrive(res.at[q_core], tok, (3,), core_dev)
    arrive(tgt.at[q_core], tok, (4,), core_dev)
    sums(q_core)
    arrive(res.at[q_far], tok, (5,), far_dev)
    arrive(tgt.at[q_far], tok, (6,), far_dev)
    sums(q_far)
    arrive(res.at[q_diag], tok, (7,), diag_dev)
    arrive(tgt.at[q_diag], tok, (8,), diag_dev)
    sums(q_diag)
    for k in range(1, Q):
        send(sm.at[q], sm.at[q], sx, (k,), group_dev(k))
    for k in range(1, Q):
        arrive(sm.at[lax.rem(q + Q - k, Q)], sx, (k,), group_dev(k))
    ssq = sm[0, 0:1, :] + sm[1, 0:1, :] + sm[2, 0:1, :] + sm[3, 0:1, :]
    shv = sm[0, 1:2, :] + sm[1, 1:2, :] + sm[2, 1:2, :] + sm[3, 1:2, :]
    token_adv = rb[1:2, :]
    valid = rb[2:3, :]
    rinv = lax.rsqrt(ssq / dw + 1e-06)
    score = shv * rinv
    ratio = jnp.exp(score - rb[0:1, :])
    plain = ratio * token_adv
    clipped = jnp.clip(ratio, 0.8, 1.2) * token_adv
    loss_local = jnp.sum(valid * -jnp.minimum(plain, clipped), axis=1, keepdims=True)
    dscore = -valid * jnp.where(plain <= clipped, plain, 0.0) / count1
    rb[3:4, :] = dscore * rinv * (32.0 * all_tokens * math.sqrt(dw))
    rb[4:5, :] = rinv * rinv * shv / dw

    row = lax.broadcasted_iota(jnp.int32, (128, tokens), 0)

    @pl.loop(0, Q)
    def _(a):
        both = jnp.where(row == 0, rb[3:4, toks_of(a)], rb[4:5, toks_of(a)]).T
        lead = both[:, 0:1]
        inner_scale = both[:, 1:2]
        v = gain[:, cols_of(q)] * tgt[a].astype(F32)
        gh[toks_of(a), :] = (lead * (v - hid[a] * inner_scale)).astype(BF16)

    ls[o, so, i] = jnp.broadcast_to(loss_local, (8, 128))
    for j in range(1, fi):
        mine = ls.at[o, so, i]
        send(mine, mine, ls2, (j,), inner_dev(j))

    def term(owner):
        return jnp.dot(ctxt[rows_of(owner), :], gh[...], preferred_element_type=F32)

    def back(a, store):
        @pl.loop(0, aw // 256)
        def _(t):
            span = pl.ds(pl.multiple_of(t * 256, 256), 256)
            store(
                span,
                lax.dot_general(gh[toks_of(a), :], w[span, :], NT, preferred_element_type=F32),
            )

    def into(ref):
        def store(span, value):
            ref[:, span] = value.astype(ref.dtype)

        return store

    order = (1, 3, 2, 0)

    def first_terms(k):
        for j in range(1, fi):
            owner = lax.rem(o + k, FO) * fi + lax.rem(i + j, fi)
            dws[k, j - 1] = term(owner).astype(BF16)
            send(dws.at[k, j - 1], irecv.at[k, j - 1], rs_i, (k, j), inner_dev(j))

    first_terms(order[0])
    back(q_diag, into(gdiag))
    send(gdiag, rdiag, gx, (0,), core_dev)
    back(q_far, into(acc))
    first_terms(order[1])
    arrive(rdiag, gx, (0,), core_dev)
    gfar[...] = (acc[...] + rdiag[...].astype(F32)).astype(BF16)
    send(gfar, rfar, gx, (1,), far_dev)
    first_terms(order[2])
    first_terms(order[3])

    @pl.loop(0, FO)
    def _(k):
        part[k] = term(lax.rem(o + k, FO) * fi + i)

    back(q_core, into(gcore))
    send(gcore, rcore, gx, (2,), core_dev)

    for j in range(1, fi):
        arrive(ls.at[o, so, lax.rem(i + fi - j, fi)], ls2, (j,), inner_dev(j))
    for m, k in outer:
        mine = ls.at[o, so]
        send(mine, mine, ls3, (m, k), outer_dev(k, m))

    def reduce_inner(k):
        for j in range(1, fi):
            arrive(irecv.at[k, j - 1], rs_i, (k, j), inner_dev(j))
        total = part[k]
        for j in range(1, fi):
            total = total + irecv[k, j - 1].astype(F32)
        if k == 0:
            part[0] = total
        if k != 0 or so_ways > 1:
            obuf[k] = total.astype(BF16)
        for m in range(so_ways):
            if (m, k) != (0, 0):
                send(obuf.at[k], orecv.at[m, k], rs_o, (m, k), outer_dev(k, m))

    reduce_inner(order[0])
    back(q, into(acc))
    reduce_inner(order[1])
    arrive(rcore, gx, (2,), core_dev)
    reduce_inner(order[2])
    reduce_inner(order[3])

    arrive(rfar, gx, (1,), far_dev)
    gfin = ctx.at[q]
    gfin[...] = (acc[...] + rcore[...].astype(F32) + rfar[...].astype(F32)).astype(BF16)
    out_ctx = local(gfin, gctx_out, 1)

    for m, k in outer:
        arrive(orecv.at[m, k], rs_o, (m, k), outer_dev(k, m))
    total = part[0] if so_ways == 1 else obuf[0].astype(F32)
    for k in range(FO):
        both = None
        for m in range(so_ways):
            if (m, k) != (0, 0):
                one = orecv[m, k].astype(F32)
                both = one if both is None else both + one
        if both is not None:
            total = total + both
    scale = 1.0 / math.sqrt(all_tokens)
    fsend[...] = (total * scale).astype(BF16)
    send(fsend, frecv.at[0], fin, (0,), far_dev)
    send(fsend, frecv.at[1], fin, (1,), core_dev)
    outs = [local(fsend, gw_out.at[:, cols_of(q)], 0)]

    for m, k in outer:
        there = ls.at[lax.rem(o + FO - k, FO), lax.rem(so + so_ways - m, so_ways)]
        arrive(there, ls3, (m, k), outer_dev(k, m))
    loss_out[...] = jnp.sum(ls[...], axis=(0, 1, 2))[0:1, 0:1] / count1

    arrive(frecv.at[1], fin, (1,), core_dev)
    outs.append(local(frecv.at[1], gw_out.at[:, cols_of(q_core)], 2))
    arrive(frecv.at[0], fin, (0,), far_dev)
    send(frecv.at[0], frecv.at[2], fin, (2,), core_dev)
    outs.append(local(frecv.at[0], gw_out.at[:, cols_of(q_far)], 3))
    arrive(frecv.at[2], fin, (2,), core_dev)
    outs.append(local(frecv.at[2], gw_out.at[:, cols_of(q_diag)], 4))
    out_ctx.wait()
    for copy in outs:
        copy.wait()
    for copy in sent:
        copy.wait_send()


def body(
    context,
    residual,
    target_rows,
    log_norm,
    norm_gain,
    out_proj,
    old_logprob,
    lengths,
    rewards,
    prompt_ids,
    placement,
):
    nrows, lmax, aw = context.shape
    dw = residual.shape[2]
    fsdp_ways = lax.axis_size("fsdp")
    seq_ways = lax.axis_size("seq")
    fi = fsdp_ways // FO
    so_ways = seq_ways // Q
    tokens = nrows * lmax
    blk = aw // fsdp_ways
    cq = dw // Q

    vmem = pl.BlockSpec(memory_space=pltpu.VMEM)
    anywhere = pl.BlockSpec(memory_space=pl.ANY)
    dma = pltpu.SemaphoreType.DMA
    buf = pltpu.VMEM
    gctx, gw, loss = pl.pallas_call(
        functools.partial(kernel, (fsdp_ways, seq_ways, nrows, lmax, dw, aw)),
        out_shape=(
            jax.ShapeDtypeStruct((tokens, aw), BF16),
            jax.ShapeDtypeStruct((blk, dw), BF16),
            jax.ShapeDtypeStruct((1, 1), F32),
        ),
        in_specs=[anywhere] * 3 + [vmem] * 2 + [anywhere] + [vmem] * 5,
        out_specs=(anywhere, anywhere, vmem),
        scratch_shapes=[
            buf((aw, cq), BF16),
            buf((Q, tokens, aw), BF16),
            buf((aw, Q * tokens), BF16),
            buf((Q, tokens, cq), BF16),
            buf((Q, tokens, cq), BF16),
            buf((Q, tokens, cq), F32),
            buf((Q * tokens, cq), BF16),
            buf((Q, 8, Q * tokens), F32),
            buf((8, Q * tokens), F32),
            buf((FO, fi - 1, blk, cq), BF16),
            buf((FO, fi - 1, blk, cq), BF16),
            buf((FO, blk, cq), F32),
            buf((FO, blk, cq), BF16),
            buf((so_ways, FO, blk, cq), BF16),
            buf((blk, cq), BF16),
            buf((3, blk, cq), BF16),
            buf((tokens, aw), F32),
            buf((tokens, aw), BF16),
            buf((tokens, aw), BF16),
            buf((tokens, aw), BF16),
            buf((tokens, aw), BF16),
            buf((tokens, aw), BF16),
            buf((tokens, aw), BF16),
            buf((FO, so_ways, fi, Q, 16, 128), F32),
            buf((FO, so_ways, fi, 8, 128), F32),
            buf((1, dw), F32),
            dma((5,)),
            dma((2, FO)),
            dma((2, FO, fi)),
            dma((2, 9)),
            dma((2, 3)),
            dma((2, Q)),
            dma((2, FO, fi)),
            dma((2, so_ways, FO)),
            dma((2, 3)),
            dma((2, Q)),
            dma((2, fi)),
            dma((2, so_ways, FO)),
            dma((2, fi)),
            dma((2, so_ways, FO)),
        ],
        compiler_params=pltpu.CompilerParams(
            collective_id=0, has_side_effects=True, vmem_limit_bytes=50 << 20
        ),
        cost_estimate=pl.CostEstimate(
            flops=6 * tokens * aw * dw, bytes_accessed=12 * tokens * dw, transcendentals=tokens
        ),
    )(
        context.reshape(tokens, aw),
        residual.reshape(tokens, dw),
        target_rows.reshape(tokens, dw),
        log_norm,
        norm_gain,
        out_proj,
        old_logprob,
        rewards.reshape(1, nrows),
        prompt_ids.reshape(1, nrows),
        lengths.reshape(1, nrows),
        placement.reshape(1, nrows),
    )
    return (gctx.reshape(nrows, lmax, aw), gw.astype(F32), loss.reshape(()))


def solution(mesh):
    return jax.shard_map(
        body,
        mesh=mesh,
        in_specs=(
            P("fsdp", "seq", None),
            P("fsdp", "seq", None),
            P("fsdp", "seq", None),
            P("fsdp", "seq"),
            P(),
            P("fsdp", None),
            P("fsdp", "seq"),
            P("fsdp", "seq"),
            P("fsdp", "seq"),
            P("fsdp", "seq"),
            P("fsdp", "seq"),
        ),
        out_specs=(P("fsdp", "seq", None), P("fsdp", None), P()),
        check_vma=False,
    )
```

```python
import functools
import math

import jax
import jax.numpy as jnp
from jax import lax
from jax.experimental import pallas as pl
from jax.experimental.pallas import tpu as pltpu
from jax.sharding import PartitionSpec as P

GS = 16
FO = 4
Q = 4
MESH = pl.DeviceIdType.MESH
F32 = jnp.float32
BF16 = jnp.bfloat16
NT = (((1,), (1,)), ((), ()))


def kernel(
    dims,
    ctx_in,
    res_in,
    tgt_in,
    lognorm,
    gain1,
    w_in,
    old,
    rewards,
    prompt_ids,
    lengths,
    placement,
    gctx_out,
    gw_out,
    loss_out,
    w,
    ctx,
    ctxt,
    res,
    tgt,
    hid,
    gh,
    sm,
    rb,
    dws,
    irecv,
    part,
    obuf,
    zr,
    mrecv,
    fsend,
    frecv,
    gwv,
    acc,
    gdiag,
    gcore,
    gfar,
    rdiag,
    rcore,
    rfar,
    pk,
    ls,
    gain,
    loc,
    ag_o,
    ag_i,
    tok,
    gx,
    sx,
    rs_i,
    rs_z,
    rs_m,
    fin,
    pk1,
    pk2,
    pk3,
    ls2,
    ls3,
):
    fsdp_ways, seq_ways, nrows, lmax, dw, aw = dims
    fi = fsdp_ways // FO
    so_ways = seq_ways // Q
    tokens = nrows * lmax
    blk = aw // fsdp_ways
    cq = dw // Q
    prompts = nrows * fsdp_ways * seq_ways // GS
    prows = max(8, prompts)
    all_tokens = tokens * fsdp_ways * seq_ways
    f = lax.axis_index("fsdp")
    s = lax.axis_index("seq")
    o = f // fi
    i = lax.rem(f, fi)
    so = s // Q
    q = lax.rem(s, Q)
    c = lax.rem(q, 2)

    def outer_dev(k, m=0):
        return (lax.rem(o + k, FO) * fi + i, lax.rem(so + m, so_ways) * Q + q)

    def inner_dev(j):
        return (o * fi + lax.rem(i + j, fi), s)

    def group_dev(k):
        return (f, so * Q + lax.rem(q + k, Q))

    q_core = q + 1 - 2 * c
    q_far = lax.rem(q + 2, Q)
    q_diag = lax.rem(q_core + 2, Q)
    core_dev = (f, so * Q + q_core)
    far_dev = (f, so * Q + q_far)
    diag_dev = (f, so * Q + q_diag)
    outer = [(m, k) for k in range(FO) for m in range(so_ways) if (m, k) != (0, 0)]
    ring = (1, 3, 2)

    def rows_of(owner):
        return pl.ds(pl.multiple_of(owner * blk, blk), blk)

    def cols_of(quarter):
        return pl.ds(pl.multiple_of(quarter * cq, 128), cq)

    def toks_of(quarter):
        return pl.ds(pl.multiple_of(quarter * tokens, 128), tokens)

    def local(src, dst, index):
        copy = pltpu.make_async_copy(src, dst, loc.at[index])
        copy.start()
        return copy

    own_w = local(w_in.at[:, cols_of(q)], w.at[rows_of(f), :], 0)
    own_ctx = local(ctx_in, ctx.at[q], 1)
    own_res = local(res_in.at[:, cols_of(q)], res.at[q], 2)
    own_tgt = local(tgt_in.at[:, cols_of(q)], tgt.at[q], 3)

    barrier = pltpu.get_barrier_semaphore()
    peers = [outer_dev(k, m) for m, k in outer]
    peers += [inner_dev(j) for j in range(1, fi)]
    peers += [group_dev(k) for k in range(1, Q)]
    for peer in peers:
        pl.semaphore_signal(barrier, inc=1, device_id=peer, device_id_type=MESH)

    at_home = (o, so, i, q)
    pk[at_home] = jnp.zeros((16, 128), F32)
    pk[at_home + (pl.ds(0, nrows), slice(None))] = old[...]
    for n, field in enumerate((rewards, prompt_ids, lengths, placement)):
        for r in range(nrows):
            pk[at_home + (pl.ds((n + 1) * nrows + r, 1), slice(None))] = jnp.broadcast_to(
                field[:, r : r + 1].astype(F32), (1, 128)
            )
    pk[at_home + (pl.ds(5 * nrows, nrows), slice(None))] = lognorm[...]
    gain[...] = gain1[...].reshape(1, dw)

    pl.semaphore_wait(barrier, len(peers))

    sent = []

    def send(src, dst, sems, index, dev):
        copy = pltpu.make_async_remote_copy(
            src_ref=src,
            dst_ref=dst,
            send_sem=sems.at[(0,) + index],
            recv_sem=sems.at[(1,) + index],
            device_id=dev,
            device_id_type=MESH,
        )
        copy.start()
        sent.append(copy)

    def arrive(dst, sems, index, dev):
        pltpu.make_async_remote_copy(
            src_ref=dst,
            dst_ref=dst,
            send_sem=sems.at[(0,) + index],
            recv_sem=sems.at[(1,) + index],
            device_id=dev,
            device_id_type=MESH,
        ).wait_recv()

    def block(owner):
        return w.at[rows_of(owner), :]

    for k in range(1, Q):
        mine = pk.at[o, so, i, q]
        send(mine, mine, pk1, (k,), group_dev(k))
    for j in range(1, fi):
        send(w_in.at[:, cols_of(q)], block(f), ag_i, (0, j), inner_dev(j))
    for k in ring:
        send(w_in.at[:, cols_of(q)], block(f), ag_o, (k,), outer_dev(k))
    send(ctx_in, ctx.at[q], tok, (0,), far_dev)
    send(ctx_in, ctx.at[q], tok, (1,), core_dev)
    send(res_in.at[:, cols_of(q_core)], res.at[q], tok, (3,), core_dev)
    send(tgt_in.at[:, cols_of(q_core)], tgt.at[q], tok, (4,), core_dev)
    send(res_in.at[:, cols_of(q_far)], res.at[q], tok, (5,), far_dev)
    send(tgt_in.at[:, cols_of(q_far)], tgt.at[q], tok, (6,), far_dev)
    send(res_in.at[:, cols_of(q_diag)], res.at[q], tok, (7,), diag_dev)
    send(tgt_in.at[:, cols_of(q_diag)], tgt.at[q], tok, (8,), diag_dev)

    def turn(a):
        @pl.loop(0, aw // 256)
        def _(t):
            span = pl.ds(pl.multiple_of(t * 256, 256), 256)
            ctxt[span, toks_of(a)] = ctx[a, :, span].T

    for k in range(1, Q):
        there = pk.at[o, so, i, lax.rem(q + Q - k, Q)]
        arrive(there, pk1, (k,), group_dev(k))
    for j in range(1, fi):
        mine = pk.at[o, so, i]
        send(mine, mine, pk2, (j,), inner_dev(j))
    own_ctx.wait()
    turn(q)
    arrive(ctx.at[q_core], tok, (1,), core_dev)
    turn(q_core)

    for j in range(1, fi):
        owner = o * fi + lax.rem(i + fi - j, fi)
        arrive(block(owner), ag_i, (0, j), inner_dev(j))
    for j in range(1, fi):
        there = pk.at[o, so, lax.rem(i + fi - j, fi)]
        arrive(there, pk2, (j,), inner_dev(j))
    for m, k in outer:
        mine = pk.at[o, so]
        send(mine, mine, pk3, (m, k), outer_dev(k, m))

    def pass_on(k):
        here = block(lax.rem(o + FO - k, FO) * fi + i)
        arrive(here, ag_o, (k,), outer_dev(k))
        for j in range(1, fi):
            send(here, here, ag_i, (k, j), inner_dev(j))

    pass_on(1)
    pass_on(3)
    arrive(ctx.at[q_far], tok, (0,), far_dev)
    send(ctx.at[q_far], ctx.at[q_far], tok, (2,), core_dev)
    pass_on(2)
    turn(q_far)
    arrive(ctx.at[q_diag], tok, (2,), core_dev)
    turn(q_diag)

    for m, k in outer:
        there = pk.at[lax.rem(o + FO - k, FO), lax.rem(so + so_ways - m, so_ways)]
        arrive(there, pk3, (m, k), outer_dev(k, m))

    prompt_row = lax.broadcasted_iota(jnp.int32, (prows, 128), 0).astype(F32)
    zero_p = jnp.zeros((prows, 128), F32)
    zero_r = jnp.zeros((1, 128), F32)

    def over_devices(fa, carry):
        for sa in range(seq_ways):
            at = (fa // fi, sa // Q, lax.rem(fa, fi), sa % Q)
            for r in range(nrows):
                gsum, gsq, count = carry
                reward = pk[at + (pl.ds(nrows + r, 1), slice(None))]
                prompt = pk[at + (pl.ds(2 * nrows + r, 1), slice(None))]
                length = pk[at + (pl.ds(3 * nrows + r, 1), slice(None))]
                hot = prompt == prompt_row
                gsum = gsum + jnp.where(hot, reward, 0.0)
                gsq = gsq + jnp.where(hot, reward * reward, 0.0)
                carry = (gsum, gsq, count + length)
        return carry

    gsum, gsq, count = lax.fori_loop(0, fsdp_ways, over_devices, (zero_p, zero_p, zero_r))
    gmean = gsum / GS
    gvar = gsq / GS - gmean * gmean
    offset = lax.broadcasted_iota(jnp.int32, (1, lmax), 1).astype(F32)
    count1 = count[:, 0:1]

    for a in range(Q):

        def over_column(fa, carry, a=a):
            at = (fa // fi, so, lax.rem(fa, fi), a)
            for r in range(nrows):
                past = pk[at + (pl.ds(r, 1), slice(None))]
                reward = pk[at + (pl.ds(nrows + r, 1), slice(None))]
                prompt = pk[at + (pl.ds(2 * nrows + r, 1), slice(None))]
                length = pk[at + (pl.ds(3 * nrows + r, 1), slice(None))]
                dest = pk[at + (pl.ds(4 * nrows + r, 1), slice(None))]
                hot = prompt == prompt_row
                mean = jnp.sum(jnp.where(hot, gmean, 0.0), axis=0, keepdims=True)
                var = jnp.sum(jnp.where(hot, gvar, 0.0), axis=0, keepdims=True)
                adv = (reward - mean) / jnp.sqrt(var + 0.25)
                fresh = []
                for j in range(nrows):
                    chosen = dest == (f * nrows + j).astype(F32)
                    l_old, l_adv, l_len = carry[3 * j : 3 * j + 3]
                    fresh += [
                        l_old + jnp.where(chosen, past, 0.0),
                        l_adv + jnp.where(chosen, adv, 0.0),
                        l_len + jnp.where(chosen, length, 0.0),
                    ]
                carry = tuple(fresh)
            return carry

        learned = lax.fori_loop(0, fsdp_ways, over_column, (zero_r,) * (3 * nrows))
        for j in range(nrows):
            l_old, l_adv, l_len = learned[3 * j : 3 * j + 3]
            at = pl.ds(a * tokens + j * lmax, lmax)
            norm = pk[o, so, i, a, pl.ds(5 * nrows + j, 1), :]
            rb[0:1, at] = norm + l_old
            rb[1:2, at] = l_adv
            rb[2:3, at] = (offset < l_len).astype(F32)

    own_w.wait()
    own_res.wait()
    own_tgt.wait()
    for k in ring:
        for j in range(1, fi):
            owner = lax.rem(o + FO - k, FO) * fi + lax.rem(i + fi - j, fi)
            arrive(block(owner), ag_i, (k, j), inner_dev(j))

    @pl.loop(0, Q)
    def _(a):
        hid[a] = jnp.dot(ctx[a], w[...], preferred_element_type=F32)

    lane = lax.broadcasted_iota(jnp.int32, (tokens, 128), 1)

    def sums(a):
        h = hid[a] + res[a].astype(F32)
        hid[a] = h
        v = gain[:, cols_of(q)] * tgt[a].astype(F32)
        ssq = jnp.sum(h * h, axis=1, keepdims=True)
        shv = jnp.sum(h * v, axis=1, keepdims=True)
        both = jnp.where(lane == 0, ssq, jnp.where(lane == 1, shv, 0.0))
        sm[q, :, toks_of(a)] = both.T[0:8, :]

    sums(q)
    arrive(res.at[q_core], tok, (3,), core_dev)
    arrive(tgt.at[q_core], tok, (4,), core_dev)
    sums(q_core)
    arrive(res.at[q_far], tok, (5,), far_dev)
    arrive(tgt.at[q_far], tok, (6,), far_dev)
    sums(q_far)
    arrive(res.at[q_diag], tok, (7,), diag_dev)
    arrive(tgt.at[q_diag], tok, (8,), diag_dev)
    sums(q_diag)
    for k in range(1, Q):
        send(sm.at[q], sm.at[q], sx, (k,), group_dev(k))
    for k in range(1, Q):
        arrive(sm.at[lax.rem(q + Q - k, Q)], sx, (k,), group_dev(k))
    ssq = sm[0, 0:1, :] + sm[1, 0:1, :] + sm[2, 0:1, :] + sm[3, 0:1, :]
    shv = sm[0, 1:2, :] + sm[1, 1:2, :] + sm[2, 1:2, :] + sm[3, 1:2, :]
    token_adv = rb[1:2, :]
    valid = rb[2:3, :]
    rinv = lax.rsqrt(ssq / dw + 1e-06)
    score = shv * rinv
    ratio = jnp.exp(score - rb[0:1, :])
    plain = ratio * token_adv
    clipped = jnp.clip(ratio, 0.8, 1.2) * token_adv
    loss_local = jnp.sum(valid * -jnp.minimum(plain, clipped), axis=1, keepdims=True)
    dscore = -valid * jnp.where(plain <= clipped, plain, 0.0) / count1
    rb[3:4, :] = dscore * rinv * (32.0 * all_tokens * math.sqrt(dw))
    rb[4:5, :] = rinv * rinv * shv / dw

    row = lax.broadcasted_iota(jnp.int32, (128, tokens), 0)

    @pl.loop(0, Q)
    def _(a):
        both = jnp.where(row == 0, rb[3:4, toks_of(a)], rb[4:5, toks_of(a)]).T
        lead = both[:, 0:1]
        inner_scale = both[:, 1:2]
        v = gain[:, cols_of(q)] * tgt[a].astype(F32)
        gh[toks_of(a), :] = (lead * (v - hid[a] * inner_scale)).astype(BF16)

    ls[o, so, i] = jnp.broadcast_to(loss_local, (8, 128))
    for j in range(1, fi):
        mine = ls.at[o, so, i]
        send(mine, mine, ls2, (j,), inner_dev(j))

    starts = ((0, 256), (256, 256), (512, cq - 512))
    pieces = [pl.ds(lo, width) for lo, width in starts]

    def term(owner, p):
        return jnp.dot(ctxt[rows_of(owner), :], gh[:, pieces[p]], preferred_element_type=F32)

    def back(a, store):
        @pl.loop(0, aw // 256)
        def _(t):
            span = pl.ds(pl.multiple_of(t * 256, 256), 256)
            store(
                span,
                lax.dot_general(gh[toks_of(a), :], w[span, :], NT, preferred_element_type=F32),
            )

    def into(ref):
        def store(span, value):
            ref[:, span] = value.astype(ref.dtype)

        return store

    oh = o // 2
    mid = lax.rem(lax.rem(o, 2) + oh, 2)
    partner = o + 1 - 2 * lax.rem(o, 2)
    dests = (3 - 3 * oh, 2 - oh, partner, o)

    def at_outer(d):
        return (d * fi + i, s)

    def first_terms(p, st):
        for j in range(1, fi):
            owner = dests[st] * fi + lax.rem(i + j, fi)
            dws[st, j - 1, :, pieces[p]] = term(owner, p).astype(BF16)
            send(
                dws.at[st, j - 1, :, pieces[p]],
                irecv.at[st, j - 1, :, pieces[p]],
                rs_i,
                (p, st, j),
                inner_dev(j),
            )

    def own_term(p, st):
        part[st, :, pieces[p]] = term(dests[st] * fi + i, p)

    def zin(p, n):
        return zr.at[n, :, pieces[p]]

    def reduce_inner(p, st):
        for j in range(1, fi):
            arrive(irecv.at[st, j - 1, :, pieces[p]], rs_i, (p, st, j), inner_dev(j))
        total = part[st, :, pieces[p]]
        for j in range(1, fi):
            total = total + irecv[st, j - 1, :, pieces[p]].astype(F32)
        if st == 3:
            part[3, :, pieces[p]] = total
            return
        obuf[st, :, pieces[p]] = total.astype(BF16)
        slot, goal = st, partner
        if st < 2:

            @pl.when(mid == 1)
            def _():
                arrive(zin(p, st), rs_z, (p, st), at_outer(partner))
                both = part[st, :, pieces[p]]
                for j in range(1, fi):
                    both = both + irecv[st, j - 1, :, pieces[p]].astype(F32)
                obuf[st, :, pieces[p]] = (both + zr[st, :, pieces[p]].astype(F32)).astype(BF16)

            slot = mid * 3 + (1 - mid) * st
            goal = mid * dests[st] + (1 - mid) * partner
        copy = pltpu.make_async_remote_copy(
            src_ref=obuf.at[st, :, pieces[p]],
            dst_ref=zr.at[slot, :, pieces[p]],
            send_sem=rs_z.at[0, p, st],
            recv_sem=rs_z.at[1, p, slot],
            device_id=at_outer(goal),
            device_id_type=MESH,
        )
        copy.start()
        sent.append(copy)

    scale = 1.0 / math.sqrt(all_tokens)
    outs = []

    def put(value, quarter, p, n):
        lo, width = starts[p]
        at = pl.ds(pl.multiple_of(quarter * cq + lo, 128), width)
        gwv[:, at] = value.astype(F32)
        outs.append(local(gwv.at[:, at], gw_out.at[:, at], 5 + 4 * p + n))

    def finish(p):
        for n in (2, 3):
            arrive(zin(p, n), rs_z, (p, n), at_outer(partner))
        total = part[3, :, pieces[p]]
        for n in (2, 3):
            total = total + zr[n, :, pieces[p]].astype(F32)
        if so_ways > 1:
            mrecv[so, :, pieces[p]] = total.astype(BF16)
            for m in range(1, so_ways):
                mine = mrecv.at[so, :, pieces[p]]
                send(mine, mine, rs_m, (p, m), outer_dev(0, m))
            for m in range(1, so_ways):
                there = mrecv.at[lax.rem(so + so_ways - m, so_ways), :, pieces[p]]
                arrive(there, rs_m, (p, m), outer_dev(0, m))
            total = mrecv[0, :, pieces[p]].astype(F32)
            for m in range(1, so_ways):
                total = total + mrecv[m, :, pieces[p]].astype(F32)
        fsend[:, pieces[p]] = (total * scale).astype(BF16)
        for n, dev in ((0, far_dev), (1, core_dev)):
            send(fsend.at[:, pieces[p]], frecv.at[n, :, pieces[p]], fin, (p, n), dev)
        put(fsend[:, pieces[p]], q, p, 0)

    def relay(p):
        arrive(frecv.at[0, :, pieces[p]], fin, (p, 0), far_dev)
        send(frecv.at[0, :, pieces[p]], frecv.at[2, :, pieces[p]], fin, (p, 2), core_dev)
        put(frecv[0, :, pieces[p]], q_far, p, 1)
        arrive(frecv.at[1, :, pieces[p]], fin, (p, 1), core_dev)
        put(frecv[1, :, pieces[p]], q_core, p, 2)

    def last(p):
        arrive(frecv.at[2, :, pieces[p]], fin, (p, 2), core_dev)
        put(frecv[2, :, pieces[p]], q_diag, p, 3)

    first_terms(0, 0)
    first_terms(0, 1)
    back(q_diag, into(gdiag))
    send(gdiag, rdiag, gx, (0,), core_dev)
    first_terms(0, 2)
    first_terms(0, 3)
    back(q_far, into(acc))
    own_term(0, 0)
    arrive(rdiag, gx, (0,), core_dev)
    gfar[...] = (acc[...] + rdiag[...].astype(F32)).astype(BF16)
    send(gfar, rfar, gx, (1,), far_dev)
    for st in range(4):
        first_terms(1, st)
    for st in range(1, 4):
        own_term(0, st)
    reduce_inner(0, 0)
    for st in range(4):
        first_terms(2, st)
    reduce_inner(0, 1)
    for st in range(4):
        own_term(1, st)
    reduce_inner(0, 2)
    for st in range(4):
        own_term(2, st)
    reduce_inner(0, 3)
    back(q_core, into(gcore))
    send(gcore, rcore, gx, (2,), core_dev)
    for j in range(1, fi):
        arrive(ls.at[o, so, lax.rem(i + fi - j, fi)], ls2, (j,), inner_dev(j))
    for m, k in outer:
        mine = ls.at[o, so]
        send(mine, mine, ls3, (m, k), outer_dev(k, m))
    back(q, into(acc))
    reduce_inner(1, 0)
    reduce_inner(1, 1)
    finish(0)
    reduce_inner(1, 2)
    reduce_inner(1, 3)
    arrive(rcore, gx, (2,), core_dev)
    acc[...] = acc[...] + rcore[...].astype(F32)
    reduce_inner(2, 0)
    reduce_inner(2, 1)
    reduce_inner(2, 2)
    finish(1)
    reduce_inner(2, 3)
    arrive(rfar, gx, (1,), far_dev)
    gfin = ctx.at[q]
    gfin[...] = (acc[...] + rfar[...].astype(F32)).astype(BF16)
    out_ctx = local(gfin, gctx_out, 1)
    finish(2)
    for m, k in outer:
        there = ls.at[lax.rem(o + FO - k, FO), lax.rem(so + so_ways - m, so_ways)]
        arrive(there, ls3, (m, k), outer_dev(k, m))
    loss_out[...] = jnp.sum(ls[...], axis=(0, 1, 2))[0:1, 0:1] / count1
    for p in range(3):
        relay(p)
        last(p)
    out_ctx.wait()
    for copy in outs:
        copy.wait()
    for copy in sent:
        copy.wait_send()


def body(
    context,
    residual,
    target_rows,
    log_norm,
    norm_gain,
    out_proj,
    old_logprob,
    lengths,
    rewards,
    prompt_ids,
    placement,
):
    nrows, lmax, aw = context.shape
    dw = residual.shape[2]
    fsdp_ways = lax.axis_size("fsdp")
    seq_ways = lax.axis_size("seq")
    fi = fsdp_ways // FO
    so_ways = seq_ways // Q
    tokens = nrows * lmax
    blk = aw // fsdp_ways
    cq = dw // Q

    vmem = pl.BlockSpec(memory_space=pltpu.VMEM)
    anywhere = pl.BlockSpec(memory_space=pl.ANY)
    dma = pltpu.SemaphoreType.DMA
    buf = pltpu.VMEM
    gctx, gw, loss = pl.pallas_call(
        functools.partial(kernel, (fsdp_ways, seq_ways, nrows, lmax, dw, aw)),
        out_shape=(
            jax.ShapeDtypeStruct((tokens, aw), BF16),
            jax.ShapeDtypeStruct((blk, dw), F32),
            jax.ShapeDtypeStruct((1, 1), F32),
        ),
        in_specs=[anywhere] * 3 + [vmem] * 2 + [anywhere] + [vmem] * 5,
        out_specs=(anywhere, anywhere, vmem),
        scratch_shapes=[
            buf((aw, cq), BF16),
            buf((Q, tokens, aw), BF16),
            buf((aw, Q * tokens), BF16),
            buf((Q, tokens, cq), BF16),
            buf((Q, tokens, cq), BF16),
            buf((Q, tokens, cq), F32),
            buf((Q * tokens, cq), BF16),
            buf((Q, 8, Q * tokens), F32),
            buf((8, Q * tokens), F32),
            buf((FO, fi - 1, blk, cq), BF16),
            buf((FO, fi - 1, blk, cq), BF16),
            buf((FO, blk, cq), F32),
            buf((3, blk, cq), BF16),
            buf((4, blk, cq), BF16),
            buf((so_ways, blk, cq), BF16),
            buf((blk, cq), BF16),
            buf((3, blk, cq), BF16),
            buf((blk, dw), F32),
            buf((tokens, aw), F32),
            buf((tokens, aw), BF16),
            buf((tokens, aw), BF16),
            buf((tokens, aw), BF16),
            buf((tokens, aw), BF16),
            buf((tokens, aw), BF16),
            buf((tokens, aw), BF16),
            buf((FO, so_ways, fi, Q, 16, 128), F32),
            buf((FO, so_ways, fi, 8, 128), F32),
            buf((1, dw), F32),
            dma((17,)),
            dma((2, FO)),
            dma((2, FO, fi)),
            dma((2, 9)),
            dma((2, 3)),
            dma((2, Q)),
            dma((2, 3, FO, fi)),
            dma((2, 3, FO)),
            dma((2, 3, so_ways)),
            dma((2, 3, 3)),
            dma((2, Q)),
            dma((2, fi)),
            dma((2, so_ways, FO)),
            dma((2, fi)),
            dma((2, so_ways, FO)),
        ],
        compiler_params=pltpu.CompilerParams(
            collective_id=0, has_side_effects=True, vmem_limit_bytes=62 << 20
        ),
        cost_estimate=pl.CostEstimate(
            flops=6 * tokens * aw * dw, bytes_accessed=12 * tokens * dw, transcendentals=tokens
        ),
    )(
        context.reshape(tokens, aw),
        residual.reshape(tokens, dw),
        target_rows.reshape(tokens, dw),
        log_norm,
        norm_gain,
        out_proj,
        old_logprob,
        rewards.reshape(1, nrows),
        prompt_ids.reshape(1, nrows),
        lengths.reshape(1, nrows),
        placement.reshape(1, nrows),
    )
    return (gctx.reshape(nrows, lmax, aw), gw, loss.reshape(()))


def solution(mesh):
    return jax.shard_map(
        body,
        mesh=mesh,
        in_specs=(
            P("fsdp", "seq", None),
            P("fsdp", "seq", None),
            P("fsdp", "seq", None),
            P("fsdp", "seq"),
            P(),
            P("fsdp", None),
            P("fsdp", "seq"),
            P("fsdp", "seq"),
            P("fsdp", "seq"),
            P("fsdp", "seq"),
            P("fsdp", "seq"),
        ),
        out_specs=(P("fsdp", "seq", None), P("fsdp", None), P()),
        check_vma=False,
    )
```

```python
import functools
import math

import jax
import jax.numpy as jnp
from jax import lax
from jax.experimental import pallas as pl
from jax.experimental.pallas import tpu as pltpu
from jax.sharding import PartitionSpec as P

GS = 16
FO = 4
Q = 4
NEAR = 128
CHUNKS = 4
VM2 = 62
MESH = pl.DeviceIdType.MESH
F32 = jnp.float32
BF16 = jnp.bfloat16
NT = (((1,), (1,)), ((), ()))


def kernel(
    dims,
    ctx_in,
    res_in,
    tgt_in,
    lognorm,
    gain1,
    w_in,
    old,
    rewards,
    prompt_ids,
    lengths,
    placement,
    gctx_out,
    gw_out,
    loss_out,
    w,
    ctx,
    ctxt,
    res,
    tgt,
    hid,
    gh,
    sm,
    rb,
    dws,
    irecv,
    part,
    obuf,
    zr,
    mrecv,
    fsend,
    frecv,
    acc,
    gdiag,
    gcore,
    gfar,
    rdiag,
    rcore,
    rfar,
    pk,
    ls,
    gain,
    gain2,
    loc,
    ag_z,
    ag_i,
    tok,
    gx,
    sx,
    rs_i,
    rs_z,
    rs_m,
    fin,
    pk1,
    pk2,
    pk3,
    ls2,
    ls3,
):
    fsdp_ways, seq_ways, nrows, lmax, dw, aw = dims
    fi = fsdp_ways // FO
    so_ways = seq_ways // Q
    tokens = nrows * lmax
    blk = aw // fsdp_ways
    cq = dw // Q
    prompts = nrows * fsdp_ways * seq_ways // GS
    prows = max(8, prompts)
    all_tokens = tokens * fsdp_ways * seq_ways
    f = lax.axis_index("fsdp")
    s = lax.axis_index("seq")
    o = f // fi
    i = lax.rem(f, fi)
    so = s // Q
    q = lax.rem(s, Q)
    c = lax.rem(q, 2)

    def outer_dev(k, m=0):
        return (lax.rem(o + k, FO) * fi + i, lax.rem(so + m, so_ways) * Q + q)

    def inner_dev(j):
        return (o * fi + lax.rem(i + j, fi), s)

    def group_dev(k):
        return (f, so * Q + lax.rem(q + k, Q))

    q_core = q + 1 - 2 * c
    q_far = lax.rem(q + 2, Q)
    q_diag = lax.rem(q_core + 2, Q)
    core_dev = (f, so * Q + q_core)
    far_dev = (f, so * Q + q_far)
    diag_dev = (f, so * Q + q_diag)
    chip = q - c
    wide = cq + NEAR
    tp = cq - NEAR
    oh = o // 2
    mid = lax.rem(lax.rem(o, 2) + oh, 2)
    partner = o + 1 - 2 * lax.rem(o, 2)
    far_mid = 2 - oh
    far_end = 3 - 3 * oh
    outer = [(m, k) for k in range(FO) for m in range(so_ways) if (m, k) != (0, 0)]

    def rows_of(owner):
        return pl.ds(pl.multiple_of(owner * blk, blk), blk)

    def cols_of(quarter):
        return pl.ds(pl.multiple_of(quarter * cq, 128), cq)

    def at_outer(d):
        return (d * fi + i, s)

    def tp_of(quarter):
        return pl.ds(pl.multiple_of(quarter * cq, 128), tp)

    def near_of(quarter):
        return pl.ds(pl.multiple_of(quarter * cq + tp, 128), NEAR)

    def toks_of(quarter):
        return pl.ds(pl.multiple_of(quarter * tokens, 128), tokens)

    def local(src, dst, index):
        copy = pltpu.make_async_copy(src, dst, loc.at[index])
        copy.start()
        return copy

    here, beyond = pl.ds(0, cq), pl.ds(cq, NEAR)
    own_w = [
        local(w_in.at[:, cols_of(q)], w.at[rows_of(f), here], 0),
        local(w_in.at[:, near_of(q_far)], w.at[rows_of(f), beyond], 1),
    ]
    own_ctx = local(ctx_in, ctx.at[q], 2)
    own_rows = [
        local(res_in.at[:, cols_of(q)], res.at[q, :, here], 3),
        local(res_in.at[:, near_of(q_far)], res.at[q, :, beyond], 4),
        local(tgt_in.at[:, cols_of(q)], tgt.at[q, :, here], 5),
        local(tgt_in.at[:, near_of(q_far)], tgt.at[q, :, beyond], 6),
    ]

    barrier = pltpu.get_barrier_semaphore()
    peers = [outer_dev(k, m) for m, k in outer]
    peers += [inner_dev(j) for j in range(1, fi)]
    peers += [group_dev(k) for k in range(1, Q)]
    for peer in peers:
        pl.semaphore_signal(barrier, inc=1, device_id=peer, device_id_type=MESH)

    at_home = (o, so, i, q)
    pk[at_home] = jnp.zeros((16, 128), F32)
    pk[at_home + (pl.ds(0, nrows), slice(None))] = old[...]
    for n, field in enumerate((rewards, prompt_ids, lengths, placement)):
        for r in range(nrows):
            pk[at_home + (pl.ds((n + 1) * nrows + r, 1), slice(None))] = jnp.broadcast_to(
                field[:, r : r + 1].astype(F32), (1, 128)
            )
    pk[at_home + (pl.ds(5 * nrows, nrows), slice(None))] = lognorm[...]
    gain[...] = gain1[...].reshape(1, dw)
    gain2[:, 0:cq] = gain[:, cols_of(q)]
    gain2[:, cq:wide] = gain[:, near_of(q_far)]

    pl.semaphore_wait(barrier, len(peers))

    sent = []

    def send(src, dst, sems, index, dev):
        copy = pltpu.make_async_remote_copy(
            src_ref=src,
            dst_ref=dst,
            send_sem=sems.at[(0,) + index],
            recv_sem=sems.at[(1,) + index],
            device_id=dev,
            device_id_type=MESH,
        )
        copy.start()
        sent.append(copy)

    def arrive(dst, sems, index, dev):
        pltpu.make_async_remote_copy(
            src_ref=dst,
            dst_ref=dst,
            send_sem=sems.at[(0,) + index],
            recv_sem=sems.at[(1,) + index],
            device_id=dev,
            device_id_type=MESH,
        ).wait_recv()

    def block(owner):
        return w.at[rows_of(owner), :]

    for k in range(1, Q):
        mine = pk.at[o, so, i, q]
        send(mine, mine, pk1, (k,), group_dev(k))
    for copy in own_w:
        copy.wait()
    for j in range(1, fi):
        send(block(f), block(f), ag_i, (3, j), inner_dev(j))

    def hop(src, n, goal):
        return pltpu.make_async_remote_copy(
            src_ref=src,
            dst_ref=src,
            send_sem=ag_z.at[0, n],
            recv_sem=ag_z.at[1, n % 3],
            device_id=at_outer(goal),
            device_id_type=MESH,
        )

    zsent = [(block(f), 4, far_mid)]

    @pl.when(mid == 1)
    def _():
        hop(*zsent[0]).start()

    send(block(f), block(f), ag_z, (0,), at_outer(partner))
    send(ctx_in, ctx.at[q], tok, (0,), far_dev)
    send(ctx_in, ctx.at[q], tok, (1,), core_dev)
    for n, (src, dst) in enumerate(((res_in, res), (tgt_in, tgt))):
        send(src.at[:, cols_of(q_core)], dst.at[q, :, here], tok, (3 + n,), core_dev)
        send(src.at[:, near_of(q_diag)], dst.at[q, :, beyond], tok, (5 + n,), core_dev)
    over = pl.ds(0, tp)
    for n, (quarter, dev) in enumerate(((q_far, far_dev), (q_diag, diag_dev))):
        send(res_in.at[:, tp_of(quarter)], res.at[q, :, over], tok, (7 + 2 * n,), dev)
        send(tgt_in.at[:, tp_of(quarter)], tgt.at[q, :, over], tok, (8 + 2 * n,), dev)

    def turn(a):
        @pl.loop(0, aw // 256)
        def _(t):
            span = pl.ds(pl.multiple_of(t * 256, 256), 256)
            ctxt[span, toks_of(a)] = ctx[a, :, span].T

    for k in range(1, Q):
        there = pk.at[o, so, i, lax.rem(q + Q - k, Q)]
        arrive(there, pk1, (k,), group_dev(k))
    for j in range(1, fi):
        mine = pk.at[o, so, i]
        send(mine, mine, pk2, (j,), inner_dev(j))
    own_ctx.wait()
    turn(q)
    for j in range(1, fi):
        there = pk.at[o, so, lax.rem(i + fi - j, fi)]
        arrive(there, pk2, (j,), inner_dev(j))
    for m, k in outer:
        mine = pk.at[o, so]
        send(mine, mine, pk3, (m, k), outer_dev(k, m))

    def pass_on(n, source, goal):
        got = block(source * fi + i)
        arrive(got, ag_z, (n,), at_outer(partner))
        onward = (got, 5 if n == 0 else n, goal)
        zsent.append(onward)

        @pl.when(mid == 1)
        def _():
            hop(*onward).start()

        for j in range(1, fi):
            send(got, got, ag_i, (n, j), inner_dev(j))

    pass_on(0, partner, far_mid)
    arrive(ctx.at[q_core], tok, (1,), core_dev)
    turn(q_core)
    pass_on(1, far_mid, partner)
    pass_on(2, far_end, partner)
    arrive(ctx.at[q_far], tok, (0,), far_dev)
    send(ctx.at[q_far], ctx.at[q_far], tok, (2,), core_dev)
    turn(q_far)
    arrive(ctx.at[q_diag], tok, (2,), core_dev)
    turn(q_diag)

    for m, k in outer:
        there = pk.at[lax.rem(o + FO - k, FO), lax.rem(so + so_ways - m, so_ways)]
        arrive(there, pk3, (m, k), outer_dev(k, m))

    prompt_row = lax.broadcasted_iota(jnp.int32, (prows, 128), 0).astype(F32)
    zero_p = jnp.zeros((prows, 128), F32)
    zero_r = jnp.zeros((1, 128), F32)

    def over_devices(fa, carry):
        for sa in range(seq_ways):
            at = (fa // fi, sa // Q, lax.rem(fa, fi), sa % Q)
            for r in range(nrows):
                gsum, gsq, count = carry
                reward = pk[at + (pl.ds(nrows + r, 1), slice(None))]
                prompt = pk[at + (pl.ds(2 * nrows + r, 1), slice(None))]
                length = pk[at + (pl.ds(3 * nrows + r, 1), slice(None))]
                hot = prompt == prompt_row
                gsum = gsum + jnp.where(hot, reward, 0.0)
                gsq = gsq + jnp.where(hot, reward * reward, 0.0)
                carry = (gsum, gsq, count + length)
        return carry

    gsum, gsq, count = lax.fori_loop(0, fsdp_ways, over_devices, (zero_p, zero_p, zero_r))
    gmean = gsum / GS
    gvar = gsq / GS - gmean * gmean
    offset = lax.broadcasted_iota(jnp.int32, (1, lmax), 1).astype(F32)
    count1 = count[:, 0:1]

    for a in range(Q):

        def over_column(fa, carry, a=a):
            at = (fa // fi, so, lax.rem(fa, fi), a)
            for r in range(nrows):
                past = pk[at + (pl.ds(r, 1), slice(None))]
                reward = pk[at + (pl.ds(nrows + r, 1), slice(None))]
                prompt = pk[at + (pl.ds(2 * nrows + r, 1), slice(None))]
                length = pk[at + (pl.ds(3 * nrows + r, 1), slice(None))]
                dest = pk[at + (pl.ds(4 * nrows + r, 1), slice(None))]
                hot = prompt == prompt_row
                mean = jnp.sum(jnp.where(hot, gmean, 0.0), axis=0, keepdims=True)
                var = jnp.sum(jnp.where(hot, gvar, 0.0), axis=0, keepdims=True)
                adv = (reward - mean) / jnp.sqrt(var + 0.25)
                fresh = []
                for j in range(nrows):
                    chosen = dest == (f * nrows + j).astype(F32)
                    l_old, l_adv, l_len = carry[3 * j : 3 * j + 3]
                    fresh += [
                        l_old + jnp.where(chosen, past, 0.0),
                        l_adv + jnp.where(chosen, adv, 0.0),
                        l_len + jnp.where(chosen, length, 0.0),
                    ]
                carry = tuple(fresh)
            return carry

        learned = lax.fori_loop(0, fsdp_ways, over_column, (zero_r,) * (3 * nrows))
        for j in range(nrows):
            l_old, l_adv, l_len = learned[3 * j : 3 * j + 3]
            at = pl.ds(a * tokens + j * lmax, lmax)
            norm = pk[o, so, i, a, pl.ds(5 * nrows + j, 1), :]
            rb[0:1, at] = norm + l_old
            rb[1:2, at] = l_adv
            rb[2:3, at] = (offset < l_len).astype(F32)

    def gathered(n, source):
        for j in range(1, fi):
            owner = source * fi + lax.rem(i + fi - j, fi)
            arrive(block(owner), ag_i, (n, j), inner_dev(j))

    def forward(first, depth, fresh):
        span = pl.ds(pl.multiple_of(first * fi * blk, 128), depth * fi * blk)

        def add(a, width):
            h = jnp.dot(ctx[a, :, span], w[span, 0:width], preferred_element_type=F32)
            hid[a, :, 0:width] = h if fresh else hid[a, :, 0:width] + h

        @pl.loop(0, 2)
        def _(t):
            add(chip + t, wide)

        @pl.loop(0, 2)
        def _(t):
            add(2 - chip + t, tp)

    gathered(3, o)
    gathered(0, partner)
    forward(2 * oh, 2, True)
    gathered(1, far_mid)
    forward(far_mid, 1, False)
    gathered(2, far_end)
    forward(far_end, 1, False)

    lane = lax.broadcasted_iota(jnp.int32, (tokens, 128), 1)

    def sums(a, width):
        h = hid[a, :, 0:width] + res[a, :, 0:width].astype(F32)
        hid[a, :, 0:width] = h
        v = gain2[:, 0:width] * tgt[a, :, 0:width].astype(F32)
        ssq = jnp.sum(h * h, axis=1, keepdims=True)
        shv = jnp.sum(h * v, axis=1, keepdims=True)
        both = jnp.where(lane == 0, ssq, jnp.where(lane == 1, shv, 0.0))
        sm[q, :, toks_of(a)] = both.T[0:8, :]

    for copy in own_rows:
        copy.wait()
    sums(q, wide)
    for n, ref in enumerate((res, tgt)):
        arrive(ref.at[q_core, :, here], tok, (3 + n,), core_dev)
        arrive(ref.at[q_core, :, beyond], tok, (5 + n,), core_dev)
    sums(q_core, wide)
    for n, (quarter, dev) in enumerate(((q_far, far_dev), (q_diag, diag_dev))):
        arrive(res.at[quarter, :, over], tok, (7 + 2 * n,), dev)
        arrive(tgt.at[quarter, :, over], tok, (8 + 2 * n,), dev)
        sums(quarter, tp)
    for k in range(1, Q):
        send(sm.at[q], sm.at[q], sx, (k,), group_dev(k))
    for k in range(1, Q):
        arrive(sm.at[lax.rem(q + Q - k, Q)], sx, (k,), group_dev(k))
    ssq = sm[0, 0:1, :] + sm[1, 0:1, :] + sm[2, 0:1, :] + sm[3, 0:1, :]
    shv = sm[0, 1:2, :] + sm[1, 1:2, :] + sm[2, 1:2, :] + sm[3, 1:2, :]
    token_adv = rb[1:2, :]
    valid = rb[2:3, :]
    rinv = lax.rsqrt(ssq / dw + 1e-06)
    score = shv * rinv
    ratio = jnp.exp(score - rb[0:1, :])
    plain = ratio * token_adv
    clipped = jnp.clip(ratio, 0.8, 1.2) * token_adv
    loss_local = jnp.sum(valid * -jnp.minimum(plain, clipped), axis=1, keepdims=True)
    dscore = -valid * jnp.where(plain <= clipped, plain, 0.0) / count1
    rb[3:4, :] = dscore * rinv * (32.0 * all_tokens * math.sqrt(dw))
    rb[4:5, :] = rinv * rinv * shv / dw

    row = lax.broadcasted_iota(jnp.int32, (128, tokens), 0)

    def make_gh(a, width):
        both = jnp.where(row == 0, rb[3:4, toks_of(a)], rb[4:5, toks_of(a)]).T
        lead = both[:, 0:1]
        inner_scale = both[:, 1:2]
        v = gain2[:, 0:width] * tgt[a, :, 0:width].astype(F32)
        gh[toks_of(a), 0:width] = (lead * (v - hid[a, :, 0:width] * inner_scale)).astype(BF16)

    @pl.loop(0, 2)
    def _(t):
        make_gh(chip + t, wide)

    def chip_rows(first):
        return pl.ds(pl.multiple_of(first * tokens, 128), 2 * tokens)

    send(
        gh.at[chip_rows(chip), beyond],
        gh.at[chip_rows(chip), pl.ds(tp, NEAR)],
        gx,
        (3,),
        far_dev,
    )

    @pl.loop(0, 2)
    def _(t):
        make_gh(2 - chip + t, tp)

    ls[o, so, i] = jnp.broadcast_to(loss_local, (8, 128))
    for j in range(1, fi):
        mine = ls.at[o, so, i]
        send(mine, mine, ls2, (j,), inner_dev(j))

    starts = ((0, 256), (256, 256), (512, cq - 512))
    pieces = [pl.ds(lo, width) for lo, width in starts]

    def term(owner, p):
        return jnp.dot(ctxt[rows_of(owner), :], gh[:, pieces[p]], preferred_element_type=F32)

    def back(a, width, store):
        @pl.loop(0, aw // 256)
        def _(t):
            span = pl.ds(pl.multiple_of(t * 256, 256), 256)
            store(
                span,
                lax.dot_general(
                    gh[toks_of(a), 0:width], w[span, 0:width], NT, preferred_element_type=F32
                ),
            )

    def into(ref):
        def store(span, value):
            ref[:, span] = value.astype(ref.dtype)

        return store

    dests = (far_end, far_mid, partner, o)

    def first_terms(p, st):
        for j in range(1, fi):
            owner = dests[st] * fi + lax.rem(i + j, fi)
            dws[st, j - 1, :, pieces[p]] = term(owner, p).astype(BF16)
            send(
                dws.at[st, j - 1, :, pieces[p]],
                irecv.at[st, j - 1, :, pieces[p]],
                rs_i,
                (p, st, j),
                inner_dev(j),
            )

    def own_term(p, st):
        part[st, :, pieces[p]] = term(dests[st] * fi + i, p)

    def zin(p, n):
        return zr.at[n, :, pieces[p]]

    def reduce_inner(p, st):
        for j in range(1, fi):
            arrive(irecv.at[st, j - 1, :, pieces[p]], rs_i, (p, st, j), inner_dev(j))
        total = part[st, :, pieces[p]]
        for j in range(1, fi):
            total = total + irecv[st, j - 1, :, pieces[p]].astype(F32)
        if st == 3:
            part[3, :, pieces[p]] = total
            return
        obuf[st, :, pieces[p]] = total.astype(BF16)
        slot, goal = st, partner
        if st < 2:

            @pl.when(mid == 1)
            def _():
                arrive(zin(p, st), rs_z, (p, st), at_outer(partner))
                both = part[st, :, pieces[p]]
                for j in range(1, fi):
                    both = both + irecv[st, j - 1, :, pieces[p]].astype(F32)
                obuf[st, :, pieces[p]] = (both + zr[st, :, pieces[p]].astype(F32)).astype(BF16)

            slot = mid * 3 + (1 - mid) * st
            goal = mid * dests[st] + (1 - mid) * partner
        copy = pltpu.make_async_remote_copy(
            src_ref=obuf.at[st, :, pieces[p]],
            dst_ref=zr.at[slot, :, pieces[p]],
            send_sem=rs_z.at[0, p, st],
            recv_sem=rs_z.at[1, p, slot],
            device_id=at_outer(goal),
            device_id_type=MESH,
        )
        copy.start()
        sent.append(copy)

    scale = 1.0 / math.sqrt(all_tokens)
    outs = []

    def put(ref, quarter, p, n):
        lo, width = starts[p]
        at = pl.ds(pl.multiple_of(quarter * cq + lo, 128), width)
        outs.append(local(ref, gw_out.at[:, at], 5 + 4 * p + n))

    def finish(p):
        for n in (2, 3):
            arrive(zin(p, n), rs_z, (p, n), at_outer(partner))
        total = part[3, :, pieces[p]]
        for n in (2, 3):
            total = total + zr[n, :, pieces[p]].astype(F32)
        if so_ways > 1:
            mrecv[so, :, pieces[p]] = total.astype(BF16)
            for m in range(1, so_ways):
                mine = mrecv.at[so, :, pieces[p]]
                send(mine, mine, rs_m, (p, m), outer_dev(0, m))
            for m in range(1, so_ways):
                there = mrecv.at[lax.rem(so + so_ways - m, so_ways), :, pieces[p]]
                arrive(there, rs_m, (p, m), outer_dev(0, m))
            total = mrecv[0, :, pieces[p]].astype(F32)
            for m in range(1, so_ways):
                total = total + mrecv[m, :, pieces[p]].astype(F32)
        fsend[:, pieces[p]] = (total * scale).astype(BF16)
        for n, dev in ((0, far_dev), (1, core_dev)):
            send(fsend.at[:, pieces[p]], frecv.at[n, :, pieces[p]], fin, (p, n), dev)
        put(fsend.at[:, pieces[p]], q, p, 0)

    def relay(p):
        arrive(frecv.at[0, :, pieces[p]], fin, (p, 0), far_dev)
        send(frecv.at[0, :, pieces[p]], frecv.at[2, :, pieces[p]], fin, (p, 2), core_dev)
        put(frecv.at[0, :, pieces[p]], q_far, p, 1)
        arrive(frecv.at[1, :, pieces[p]], fin, (p, 1), core_dev)
        put(frecv.at[1, :, pieces[p]], q_core, p, 2)

    def last(p):
        arrive(frecv.at[2, :, pieces[p]], fin, (p, 2), core_dev)
        put(frecv.at[2, :, pieces[p]], q_diag, p, 3)

    first_terms(0, 0)
    first_terms(0, 1)
    back(q_diag, tp, into(gdiag))
    send(gdiag, rdiag, gx, (0,), core_dev)
    first_terms(0, 2)
    first_terms(0, 3)
    back(q_far, tp, into(acc))
    own_term(0, 0)
    arrive(rdiag, gx, (0,), core_dev)
    gfar[...] = (acc[...] + rdiag[...].astype(F32)).astype(BF16)
    send(gfar, rfar, gx, (1,), far_dev)
    for st in range(4):
        first_terms(1, st)
    for st in range(1, 4):
        own_term(0, st)
    reduce_inner(0, 0)
    arrive(gh.at[chip_rows(2 - chip), pl.ds(tp, NEAR)], gx, (3,), far_dev)
    for st in range(4):
        first_terms(2, st)
    reduce_inner(0, 1)
    for st in range(4):
        own_term(1, st)
    reduce_inner(0, 2)
    for st in range(4):
        own_term(2, st)
    reduce_inner(0, 3)
    back(q_core, wide, into(gcore))
    send(gcore, rcore, gx, (2,), core_dev)
    for j in range(1, fi):
        arrive(ls.at[o, so, lax.rem(i + fi - j, fi)], ls2, (j,), inner_dev(j))
    for m, k in outer:
        mine = ls.at[o, so]
        send(mine, mine, ls3, (m, k), outer_dev(k, m))
    back(q, wide, into(acc))
    reduce_inner(1, 0)
    reduce_inner(1, 1)
    finish(0)
    reduce_inner(1, 2)
    reduce_inner(1, 3)
    arrive(rcore, gx, (2,), core_dev)
    acc[...] = acc[...] + rcore[...].astype(F32)
    reduce_inner(2, 0)
    reduce_inner(2, 1)
    reduce_inner(2, 2)
    finish(1)
    reduce_inner(2, 3)
    arrive(rfar, gx, (1,), far_dev)
    gfin = ctx.at[q]
    gfin[...] = (acc[...] + rfar[...].astype(F32)).astype(BF16)
    out_ctx = local(gfin, gctx_out, 1)
    finish(2)
    for m, k in outer:
        there = ls.at[lax.rem(o + FO - k, FO), lax.rem(so + so_ways - m, so_ways)]
        arrive(there, ls3, (m, k), outer_dev(k, m))
    loss_out[...] = jnp.sum(ls[...], axis=(0, 1, 2))[0:1, 0:1] / count1
    for p in range(3):
        relay(p)
        last(p)
    out_ctx.wait()
    for copy in outs:
        copy.wait()
    for copy in sent:
        copy.wait_send()

    @pl.when(mid == 1)
    def _():
        for onward in zsent:
            hop(*onward).wait_send()


def hand_over(gctx_in, gw_in, gctx_out, gw_out, gctx, gw, gw32, sems):
    def parts_of(ref):
        step = ref.shape[1] // CHUNKS
        return [(slice(None), pl.ds(n * step, step)) for n in range(CHUNKS)]

    def copies(src, dst, kind):
        return [
            pltpu.make_async_copy(src.at[at], dst.at[at], sems.at[kind, n])
            for n, at in enumerate(parts_of(src))
        ]

    gw_loads = copies(gw_in, gw, 0)
    gctx_loads = copies(gctx_in, gctx, 1)
    gw_stores = copies(gw32, gw_out, 2)
    gctx_stores = copies(gctx, gctx_out, 3)
    for one, two in zip(gw_loads, gctx_loads):
        one.start()
        two.start()
    for n, at in enumerate(parts_of(gw)):
        gw_loads[n].wait()
        gw32[at] = gw[at].astype(F32)
        gw_stores[n].start()
        gctx_loads[n].wait()
        gctx_stores[n].start()
    for copy in gw_stores + gctx_stores:
        copy.wait()


def body(
    context,
    residual,
    target_rows,
    log_norm,
    norm_gain,
    out_proj,
    old_logprob,
    lengths,
    rewards,
    prompt_ids,
    placement,
):
    nrows, lmax, aw = context.shape
    dw = residual.shape[2]
    fsdp_ways = lax.axis_size("fsdp")
    seq_ways = lax.axis_size("seq")
    fi = fsdp_ways // FO
    so_ways = seq_ways // Q
    tokens = nrows * lmax
    blk = aw // fsdp_ways
    cq = dw // Q
    wide = cq + NEAR

    vmem = pl.BlockSpec(memory_space=pltpu.VMEM)
    anywhere = pl.BlockSpec(memory_space=pl.ANY)
    dma = pltpu.SemaphoreType.DMA
    buf = pltpu.VMEM
    gctx, gw, loss = pl.pallas_call(
        functools.partial(kernel, (fsdp_ways, seq_ways, nrows, lmax, dw, aw)),
        out_shape=(
            jax.ShapeDtypeStruct((tokens, aw), BF16),
            jax.ShapeDtypeStruct((blk, dw), BF16),
            jax.ShapeDtypeStruct((1, 1), F32),
        ),
        in_specs=[anywhere] * 3 + [vmem] * 2 + [anywhere] + [vmem] * 5,
        out_specs=(anywhere, anywhere, vmem),
        scratch_shapes=[
            buf((aw, wide), BF16),
            buf((Q, tokens, aw), BF16),
            buf((aw, Q * tokens), BF16),
            buf((Q, tokens, wide), BF16),
            buf((Q, tokens, wide), BF16),
            buf((Q, tokens, wide), F32),
            buf((Q * tokens, wide), BF16),
            buf((Q, 8, Q * tokens), F32),
            buf((8, Q * tokens), F32),
            buf((FO, fi - 1, blk, cq), BF16),
            buf((FO, fi - 1, blk, cq), BF16),
            buf((FO, blk, cq), F32),
            buf((3, blk, cq), BF16),
            buf((4, blk, cq), BF16),
            buf((so_ways, blk, cq), BF16),
            buf((blk, cq), BF16),
            buf((3, blk, cq), BF16),
            buf((tokens, aw), F32),
            buf((tokens, aw), BF16),
            buf((tokens, aw), BF16),
            buf((tokens, aw), BF16),
            buf((tokens, aw), BF16),
            buf((tokens, aw), BF16),
            buf((tokens, aw), BF16),
            buf((FO, so_ways, fi, Q, 16, 128), F32),
            buf((FO, so_ways, fi, 8, 128), F32),
            buf((1, dw), F32),
            buf((1, wide), F32),
            dma((17,)),
            dma((2, 6)),
            dma((2, 4, fi)),
            dma((2, 11)),
            dma((2, 4)),
            dma((2, Q)),
            dma((2, 3, FO, fi)),
            dma((2, 3, FO)),
            dma((2, 3, so_ways)),
            dma((2, 3, 3)),
            dma((2, Q)),
            dma((2, fi)),
            dma((2, so_ways, FO)),
            dma((2, fi)),
            dma((2, so_ways, FO)),
        ],
        compiler_params=pltpu.CompilerParams(
            collective_id=0, has_side_effects=True, vmem_limit_bytes=62 << 20
        ),
        cost_estimate=pl.CostEstimate(
            flops=6 * tokens * aw * dw, bytes_accessed=12 * tokens * dw, transcendentals=tokens
        ),
    )(
        context.reshape(tokens, aw),
        residual.reshape(tokens, dw),
        target_rows.reshape(tokens, dw),
        log_norm,
        norm_gain,
        out_proj,
        old_logprob,
        rewards.reshape(1, nrows),
        prompt_ids.reshape(1, nrows),
        lengths.reshape(1, nrows),
        placement.reshape(1, nrows),
    )
    gctx, gw = pl.pallas_call(
        hand_over,
        out_shape=(
            jax.ShapeDtypeStruct((tokens, aw), BF16),
            jax.ShapeDtypeStruct((blk, dw), F32),
        ),
        in_specs=[anywhere] * 2,
        out_specs=(anywhere,) * 2,
        scratch_shapes=[
            buf((tokens, aw), BF16),
            buf((blk, dw), BF16),
            buf((blk, dw), F32),
            dma((4, CHUNKS)),
        ],
        compiler_params=pltpu.CompilerParams(vmem_limit_bytes=VM2 << 20),
        cost_estimate=pl.CostEstimate(
            flops=blk * dw, bytes_accessed=4 * tokens * aw + 6 * blk * dw, transcendentals=0
        ),
    )(gctx, gw)
    return (gctx.reshape(nrows, lmax, aw), gw, loss.reshape(()))


def solution(mesh):
    return jax.shard_map(
        body,
        mesh=mesh,
        in_specs=(
            P("fsdp", "seq", None),
            P("fsdp", "seq", None),
            P("fsdp", "seq", None),
            P("fsdp", "seq"),
            P(),
            P("fsdp", None),
            P("fsdp", "seq"),
            P("fsdp", "seq"),
            P("fsdp", "seq"),
            P("fsdp", "seq"),
            P("fsdp", "seq"),
        ),
        out_specs=(P("fsdp", "seq", None), P("fsdp", None), P()),
        check_vma=False,
    )
```

```python
import functools
import math

import jax
import jax.numpy as jnp
from jax import lax
from jax.experimental import pallas as pl
from jax.experimental.pallas import tpu as pltpu
from jax.sharding import PartitionSpec as P

GS = 16
FO = 4
Q = 4
NEAR = 128
CHUNKS = 4
VM2 = 62
MESH = pl.DeviceIdType.MESH
F32 = jnp.float32
BF16 = jnp.bfloat16
NT = (((1,), (1,)), ((), ()))


def kernel(
    dims,
    ctx_in,
    res_in,
    tgt_in,
    lognorm_in,
    gain_in,
    w_in,
    old_in,
    rewards_in,
    prompt_ids_in,
    lengths_in,
    placement_in,
    gctx_out,
    gw_out,
    loss_out,
    w,
    ctx,
    ctxt,
    res,
    tgt,
    hid,
    gh,
    sm,
    rb,
    dws,
    irecv,
    part,
    obuf,
    zr,
    mrecv,
    fsend,
    frecv,
    acc,
    gdiag,
    gcore,
    gfar,
    rdiag,
    rcore,
    rfar,
    pk,
    ls,
    gain,
    gain2,
    lognorm,
    gain1,
    old,
    rewards,
    prompt_ids,
    lengths,
    placement,
    loc,
    ag_z,
    ag_i,
    tok,
    gx,
    sx,
    rs_i,
    rs_z,
    rs_m,
    fin,
    pk1,
    pk2,
    pk3,
    ls2,
    ls3,
):
    fsdp_ways, seq_ways, nrows, lmax, dw, aw = dims
    fi = fsdp_ways // FO
    so_ways = seq_ways // Q
    tokens = nrows * lmax
    blk = aw // fsdp_ways
    cq = dw // Q
    prompts = nrows * fsdp_ways * seq_ways // GS
    prows = max(8, prompts)
    all_tokens = tokens * fsdp_ways * seq_ways
    f = lax.axis_index("fsdp")
    s = lax.axis_index("seq")
    o = f // fi
    i = lax.rem(f, fi)
    so = s // Q
    q = lax.rem(s, Q)
    c = lax.rem(q, 2)

    def outer_dev(k, m=0):
        return (lax.rem(o + k, FO) * fi + i, lax.rem(so + m, so_ways) * Q + q)

    def inner_dev(j):
        return (o * fi + lax.rem(i + j, fi), s)

    def group_dev(k):
        return (f, so * Q + lax.rem(q + k, Q))

    q_core = q + 1 - 2 * c
    q_far = lax.rem(q + 2, Q)
    q_diag = lax.rem(q_core + 2, Q)
    core_dev = (f, so * Q + q_core)
    far_dev = (f, so * Q + q_far)
    diag_dev = (f, so * Q + q_diag)
    chip = q - c
    wide = cq + NEAR
    tp = cq - NEAR
    oh = o // 2
    mid = lax.rem(lax.rem(o, 2) + oh, 2)
    partner = o + 1 - 2 * lax.rem(o, 2)
    far_mid = 2 - oh
    far_end = 3 - 3 * oh
    outer = [(m, k) for k in range(FO) for m in range(so_ways) if (m, k) != (0, 0)]

    def rows_of(owner):
        return pl.ds(pl.multiple_of(owner * blk, blk), blk)

    def cols_of(quarter):
        return pl.ds(pl.multiple_of(quarter * cq, 128), cq)

    def at_outer(d):
        return (d * fi + i, s)

    def tp_of(quarter):
        return pl.ds(pl.multiple_of(quarter * cq, 128), tp)

    def near_of(quarter):
        return pl.ds(pl.multiple_of(quarter * cq + tp, 128), NEAR)

    def toks_of(quarter):
        return pl.ds(pl.multiple_of(quarter * tokens, 128), tokens)

    def local(src, dst, index):
        copy = pltpu.make_async_copy(src, dst, loc.at[index])
        copy.start()
        return copy

    barrier = pltpu.get_barrier_semaphore()
    peers = [outer_dev(k, m) for m, k in outer] if so_ways > 1 else [at_outer(partner)]
    peers += [inner_dev(j) for j in range(1, fi)]
    peers += [group_dev(k) for k in range(1, Q)]
    for peer in peers:
        pl.semaphore_signal(barrier, inc=1, device_id=peer, device_id_type=MESH)
    if so_ways == 1:

        @pl.when(mid == 1)
        def _():
            pl.semaphore_signal(
                barrier, inc=1, device_id=at_outer(far_mid), device_id_type=MESH
            )


    small = [
        local(src, dst, 7 + n)
        for n, (src, dst) in enumerate(
            (
                (old_in, old),
                (rewards_in, rewards),
                (prompt_ids_in, prompt_ids),
                (lengths_in, lengths),
                (placement_in, placement),
                (lognorm_in, lognorm),
                (gain_in, gain1),
            )
        )
    ]
    here, beyond = pl.ds(0, cq), pl.ds(cq, NEAR)
    own_w = [
        local(w_in.at[:, cols_of(q)], w.at[rows_of(f), here], 0),
        local(w_in.at[:, near_of(q_far)], w.at[rows_of(f), beyond], 1),
    ]
    own_ctx = local(ctx_in, ctx.at[q], 2)
    own_rows = [
        local(res_in.at[:, cols_of(q)], res.at[q, :, here], 3),
        local(res_in.at[:, near_of(q_far)], res.at[q, :, beyond], 4),
        local(tgt_in.at[:, cols_of(q)], tgt.at[q, :, here], 5),
        local(tgt_in.at[:, near_of(q_far)], tgt.at[q, :, beyond], 6),
    ]

    for copy in small:
        copy.wait()
    at_home = (o, so, i, q)
    pk[at_home] = jnp.zeros((16, 128), F32)
    pk[at_home + (pl.ds(0, nrows), slice(None))] = old[...]
    for n, field in enumerate((rewards, prompt_ids, lengths, placement)):
        for r in range(nrows):
            pk[at_home + (pl.ds((n + 1) * nrows + r, 1), slice(None))] = jnp.broadcast_to(
                field[:, r : r + 1].astype(F32), (1, 128)
            )
    pk[at_home + (pl.ds(5 * nrows, nrows), slice(None))] = lognorm[...]
    gain[...] = gain1[...].reshape(1, dw)
    gain2[:, 0:cq] = gain[:, cols_of(q)]
    gain2[:, cq:wide] = gain[:, near_of(q_far)]

    pl.semaphore_wait(barrier, len(peers) + (mid if so_ways == 1 else 0))

    sent = []

    def send(src, dst, sems, index, dev):
        copy = pltpu.make_async_remote_copy(
            src_ref=src,
            dst_ref=dst,
            send_sem=sems.at[(0,) + index],
            recv_sem=sems.at[(1,) + index],
            device_id=dev,
            device_id_type=MESH,
        )
        copy.start()
        sent.append(copy)

    def arrive(dst, sems, index, dev):
        pltpu.make_async_remote_copy(
            src_ref=dst,
            dst_ref=dst,
            send_sem=sems.at[(0,) + index],
            recv_sem=sems.at[(1,) + index],
            device_id=dev,
            device_id_type=MESH,
        ).wait_recv()

    cut = (blk // 2 + 15) // 16 * 16
    row_halves = ((0, cut), (cut, blk - cut))

    def block(owner, h):
        first, count = row_halves[h]
        return w.at[pl.ds(pl.multiple_of(owner * blk + first, 16), count), :]

    for k in range(1, Q):
        mine = pk.at[o, so, i, q]
        send(mine, mine, pk1, (k,), group_dev(k))
    for copy in own_w:
        copy.wait()
    for h in range(2):
        for j in range(1, fi):
            send(block(f, h), block(f, h), ag_i, (3, h, j), inner_dev(j))

    def hop(src, n, h, goal):
        return pltpu.make_async_remote_copy(
            src_ref=src,
            dst_ref=src,
            send_sem=ag_z.at[0, n, h],
            recv_sem=ag_z.at[1, n % 3, h],
            device_id=at_outer(goal),
            device_id_type=MESH,
        )

    zsent = [(block(f, h), 4, h, far_mid) for h in range(2)]

    @pl.when(mid == 1)
    def _():
        for onward in zsent[:2]:
            hop(*onward).start()

    for h in range(2):
        send(block(f, h), block(f, h), ag_z, (0, h), at_outer(partner))
    send(ctx_in, ctx.at[q], tok, (0,), far_dev)
    send(ctx_in, ctx.at[q], tok, (1,), core_dev)
    for n, (src, dst) in enumerate(((res_in, res), (tgt_in, tgt))):
        send(src.at[:, cols_of(q_core)], dst.at[q, :, here], tok, (3 + n,), core_dev)
        send(src.at[:, near_of(q_diag)], dst.at[q, :, beyond], tok, (5 + n,), core_dev)
    over = pl.ds(0, tp)
    for n, (quarter, dev) in enumerate(((q_far, far_dev), (q_diag, diag_dev))):
        send(res_in.at[:, tp_of(quarter)], res.at[q, :, over], tok, (7 + 2 * n,), dev)
        send(tgt_in.at[:, tp_of(quarter)], tgt.at[q, :, over], tok, (8 + 2 * n,), dev)

    def turn(a):
        @pl.loop(0, aw // 256)
        def _(t):
            span = pl.ds(pl.multiple_of(t * 256, 256), 256)
            ctxt[span, toks_of(a)] = ctx[a, :, span].T

    for k in range(1, Q):
        there = pk.at[o, so, i, lax.rem(q + Q - k, Q)]
        arrive(there, pk1, (k,), group_dev(k))
    for j in range(1, fi):
        mine = pk.at[o, so, i]
        send(mine, mine, pk2, (j,), inner_dev(j))
    own_ctx.wait()
    turn(q)
    for j in range(1, fi):
        there = pk.at[o, so, lax.rem(i + fi - j, fi)]
        arrive(there, pk2, (j,), inner_dev(j))

    def pass_half(n, h, source, goal):
        got = block(source * fi + i, h)
        arrive(got, ag_z, (n, h), at_outer(partner))
        onward = (got, 5 if n == 0 else n, h, goal)
        zsent.append(onward)

        @pl.when(mid == 1)
        def _():
            hop(*onward).start()

        for j in range(1, fi):
            send(got, got, ag_i, (n, h, j), inner_dev(j))

    def pass_on(n, source, goal):
        for h in range(2):
            pass_half(n, h, source, goal)

    pass_on(0, partner, far_mid)
    arrive(ctx.at[q_core], tok, (1,), core_dev)
    turn(q_core)
    pass_on(1, far_mid, partner)
    pass_on(2, far_end, partner)
    for m, k in outer:
        mine = pk.at[o, so]
        send(mine, mine, pk3, (m, k), outer_dev(k, m))
    arrive(ctx.at[q_far], tok, (0,), far_dev)
    send(ctx.at[q_far], ctx.at[q_far], tok, (2,), core_dev)
    turn(q_far)
    arrive(ctx.at[q_diag], tok, (2,), core_dev)
    turn(q_diag)

    def gathered(n, source):
        for j in range(1, fi):
            owner = source * fi + lax.rem(i + fi - j, fi)
            for h in range(2):
                arrive(block(owner, h), ag_i, (n, h, j), inner_dev(j))

    def forward(first, depth, fresh):
        span = pl.ds(pl.multiple_of(first * fi * blk, 128), depth * fi * blk)

        def add(a, width):
            h = jnp.dot(ctx[a, :, span], w[span, 0:width], preferred_element_type=F32)
            hid[a, :, 0:width] = h if fresh else hid[a, :, 0:width] + h

        @pl.loop(0, 2)
        def _(t):
            add(chip + t, wide)

        @pl.loop(0, 2)
        def _(t):
            add(2 - chip + t, tp)

    gathered(3, o)
    gathered(0, partner)
    forward(2 * oh, 2, True)
    for m, k in outer:
        there = pk.at[lax.rem(o + FO - k, FO), lax.rem(so + so_ways - m, so_ways)]
        arrive(there, pk3, (m, k), outer_dev(k, m))

    prompt_row = lax.broadcasted_iota(jnp.int32, (prows, 128), 0).astype(F32)
    zero_p = jnp.zeros((prows, 128), F32)
    zero_r = jnp.zeros((1, 128), F32)

    def over_devices(fa, carry):
        for sa in range(seq_ways):
            at = (fa // fi, sa // Q, lax.rem(fa, fi), sa % Q)
            for r in range(nrows):
                gsum, gsq, count = carry
                reward = pk[at + (pl.ds(nrows + r, 1), slice(None))]
                prompt = pk[at + (pl.ds(2 * nrows + r, 1), slice(None))]
                length = pk[at + (pl.ds(3 * nrows + r, 1), slice(None))]
                hot = prompt == prompt_row
                gsum = gsum + jnp.where(hot, reward, 0.0)
                gsq = gsq + jnp.where(hot, reward * reward, 0.0)
                carry = (gsum, gsq, count + length)
        return carry

    gsum, gsq, count = lax.fori_loop(0, fsdp_ways, over_devices, (zero_p, zero_p, zero_r))
    gmean = gsum / GS
    gvar = gsq / GS - gmean * gmean
    offset = lax.broadcasted_iota(jnp.int32, (1, lmax), 1).astype(F32)
    count1 = count[:, 0:1]

    for a in range(Q):

        def over_column(fa, carry, a=a):
            at = (fa // fi, so, lax.rem(fa, fi), a)
            for r in range(nrows):
                past = pk[at + (pl.ds(r, 1), slice(None))]
                reward = pk[at + (pl.ds(nrows + r, 1), slice(None))]
                prompt = pk[at + (pl.ds(2 * nrows + r, 1), slice(None))]
                length = pk[at + (pl.ds(3 * nrows + r, 1), slice(None))]
                dest = pk[at + (pl.ds(4 * nrows + r, 1), slice(None))]
                hot = prompt == prompt_row
                mean = jnp.sum(jnp.where(hot, gmean, 0.0), axis=0, keepdims=True)
                var = jnp.sum(jnp.where(hot, gvar, 0.0), axis=0, keepdims=True)
                adv = (reward - mean) / jnp.sqrt(var + 0.25)
                fresh = []
                for j in range(nrows):
                    chosen = dest == (f * nrows + j).astype(F32)
                    l_old, l_adv, l_len = carry[3 * j : 3 * j + 3]
                    fresh += [
                        l_old + jnp.where(chosen, past, 0.0),
                        l_adv + jnp.where(chosen, adv, 0.0),
                        l_len + jnp.where(chosen, length, 0.0),
                    ]
                carry = tuple(fresh)
            return carry

        learned = lax.fori_loop(0, fsdp_ways, over_column, (zero_r,) * (3 * nrows))
        for j in range(nrows):
            l_old, l_adv, l_len = learned[3 * j : 3 * j + 3]
            at = pl.ds(a * tokens + j * lmax, lmax)
            norm = pk[o, so, i, a, pl.ds(5 * nrows + j, 1), :]
            rb[0:1, at] = norm + l_old
            rb[1:2, at] = l_adv
            rb[2:3, at] = (offset < l_len).astype(F32)

    gathered(1, far_mid)
    forward(far_mid, 1, False)
    gathered(2, far_end)
    forward(far_end, 1, False)

    lane = lax.broadcasted_iota(jnp.int32, (tokens, 128), 1)

    def sums(a, width):
        h = hid[a, :, 0:width] + res[a, :, 0:width].astype(F32)
        hid[a, :, 0:width] = h
        v = gain2[:, 0:width] * tgt[a, :, 0:width].astype(F32)
        ssq = jnp.sum(h * h, axis=1, keepdims=True)
        shv = jnp.sum(h * v, axis=1, keepdims=True)
        both = jnp.where(lane == 0, ssq, jnp.where(lane == 1, shv, 0.0))
        sm[q, :, toks_of(a)] = both.T[0:8, :]

    for copy in own_rows:
        copy.wait()
    sums(q, wide)
    for n, ref in enumerate((res, tgt)):
        arrive(ref.at[q_core, :, here], tok, (3 + n,), core_dev)
        arrive(ref.at[q_core, :, beyond], tok, (5 + n,), core_dev)
    sums(q_core, wide)
    for n, (quarter, dev) in enumerate(((q_far, far_dev), (q_diag, diag_dev))):
        arrive(res.at[quarter, :, over], tok, (7 + 2 * n,), dev)
        arrive(tgt.at[quarter, :, over], tok, (8 + 2 * n,), dev)
        sums(quarter, tp)
    for k in range(1, Q):
        send(sm.at[q], sm.at[q], sx, (k,), group_dev(k))
    for k in range(1, Q):
        arrive(sm.at[lax.rem(q + Q - k, Q)], sx, (k,), group_dev(k))
    ssq = sm[0, 0:1, :] + sm[1, 0:1, :] + sm[2, 0:1, :] + sm[3, 0:1, :]
    shv = sm[0, 1:2, :] + sm[1, 1:2, :] + sm[2, 1:2, :] + sm[3, 1:2, :]
    token_adv = rb[1:2, :]
    valid = rb[2:3, :]
    rinv = lax.rsqrt(ssq / dw + 1e-06)
    score = shv * rinv
    ratio = jnp.exp(score - rb[0:1, :])
    plain = ratio * token_adv
    clipped = jnp.clip(ratio, 0.8, 1.2) * token_adv
    loss_local = jnp.sum(valid * -jnp.minimum(plain, clipped), axis=1, keepdims=True)
    dscore = -valid * jnp.where(plain <= clipped, plain, 0.0) / count1
    rb[3:4, :] = dscore * rinv * (32.0 * all_tokens * math.sqrt(dw))
    rb[4:5, :] = rinv * rinv * shv / dw

    row = lax.broadcasted_iota(jnp.int32, (128, tokens), 0)

    def make_gh(a, width):
        both = jnp.where(row == 0, rb[3:4, toks_of(a)], rb[4:5, toks_of(a)]).T
        lead = both[:, 0:1]
        inner_scale = both[:, 1:2]
        v = gain2[:, 0:width] * tgt[a, :, 0:width].astype(F32)
        gh[toks_of(a), 0:width] = (lead * (v - hid[a, :, 0:width] * inner_scale)).astype(BF16)

    @pl.loop(0, 2)
    def _(t):
        make_gh(chip + t, wide)

    def chip_rows(first):
        return pl.ds(pl.multiple_of(first * tokens, 128), 2 * tokens)

    send(
        gh.at[chip_rows(chip), beyond],
        gh.at[chip_rows(chip), pl.ds(tp, NEAR)],
        gx,
        (3,),
        far_dev,
    )

    @pl.loop(0, 2)
    def _(t):
        make_gh(2 - chip + t, tp)

    ls[o, so, i] = jnp.broadcast_to(loss_local, (8, 128))
    for j in range(1, fi):
        mine = ls.at[o, so, i]
        send(mine, mine, ls2, (j,), inner_dev(j))

    starts = ((0, 256), (256, 256), (512, cq - 512))
    pieces = [pl.ds(lo, width) for lo, width in starts]

    def term(owner, p):
        return jnp.dot(ctxt[rows_of(owner), :], gh[:, pieces[p]], preferred_element_type=F32)

    steps = aw // 256
    halves = ((0, steps // 2), (steps // 2, steps))

    def back(a, width, store, lo=0, hi=steps):
        @pl.loop(lo, hi)
        def _(t):
            span = pl.ds(pl.multiple_of(t * 256, 256), 256)
            store(
                span,
                lax.dot_general(
                    gh[toks_of(a), 0:width], w[span, 0:width], NT, preferred_element_type=F32
                ),
            )

    def into(ref):
        def store(span, value):
            ref[:, span] = value.astype(ref.dtype)

        return store

    dests = (far_end, far_mid, partner, o)

    def first_terms(p, st):
        for j in range(1, fi):
            owner = dests[st] * fi + lax.rem(i + j, fi)
            dws[st, j - 1, :, pieces[p]] = term(owner, p).astype(BF16)
            send(
                dws.at[st, j - 1, :, pieces[p]],
                irecv.at[st, j - 1, :, pieces[p]],
                rs_i,
                (p, st, j),
                inner_dev(j),
            )

    def own_term(p, st):
        part[st, :, pieces[p]] = term(dests[st] * fi + i, p)

    def zin(p, n):
        return zr.at[n, :, pieces[p]]

    def reduce_inner(p, st):
        for j in range(1, fi):
            arrive(irecv.at[st, j - 1, :, pieces[p]], rs_i, (p, st, j), inner_dev(j))
        total = part[st, :, pieces[p]]
        for j in range(1, fi):
            total = total + irecv[st, j - 1, :, pieces[p]].astype(F32)
        if st == 3:
            part[3, :, pieces[p]] = total
            return
        obuf[st, :, pieces[p]] = total.astype(BF16)
        slot, goal = st, partner
        if st < 2:

            @pl.when(mid == 1)
            def _():
                arrive(zin(p, st), rs_z, (p, st), at_outer(partner))
                both = part[st, :, pieces[p]]
                for j in range(1, fi):
                    both = both + irecv[st, j - 1, :, pieces[p]].astype(F32)
                obuf[st, :, pieces[p]] = (both + zr[st, :, pieces[p]].astype(F32)).astype(BF16)

            slot = mid * 3 + (1 - mid) * st
            goal = mid * dests[st] + (1 - mid) * partner
        copy = pltpu.make_async_remote_copy(
            src_ref=obuf.at[st, :, pieces[p]],
            dst_ref=zr.at[slot, :, pieces[p]],
            send_sem=rs_z.at[0, p, st],
            recv_sem=rs_z.at[1, p, slot],
            device_id=at_outer(goal),
            device_id_type=MESH,
        )
        copy.start()
        sent.append(copy)

    scale = 1.0 / math.sqrt(all_tokens)
    outs = []

    def put(ref, quarter, p, n):
        lo, width = starts[p]
        at = pl.ds(pl.multiple_of(quarter * cq + lo, 128), width)
        outs.append(local(ref, gw_out.at[:, at], 5 + 4 * p + n))

    def finish(p):
        for n in (2, 3):
            arrive(zin(p, n), rs_z, (p, n), at_outer(partner))
        total = part[3, :, pieces[p]]
        for n in (2, 3):
            total = total + zr[n, :, pieces[p]].astype(F32)
        if so_ways > 1:
            mrecv[so, :, pieces[p]] = total.astype(BF16)
            for m in range(1, so_ways):
                mine = mrecv.at[so, :, pieces[p]]
                send(mine, mine, rs_m, (p, m), outer_dev(0, m))
            for m in range(1, so_ways):
                there = mrecv.at[lax.rem(so + so_ways - m, so_ways), :, pieces[p]]
                arrive(there, rs_m, (p, m), outer_dev(0, m))
            total = mrecv[0, :, pieces[p]].astype(F32)
            for m in range(1, so_ways):
                total = total + mrecv[m, :, pieces[p]].astype(F32)
        fsend[:, pieces[p]] = (total * scale).astype(BF16)
        for n, dev in ((0, far_dev), (1, core_dev)):
            send(fsend.at[:, pieces[p]], frecv.at[n, :, pieces[p]], fin, (p, n), dev)
        put(fsend.at[:, pieces[p]], q, p, 0)

    def relay(p):
        arrive(frecv.at[0, :, pieces[p]], fin, (p, 0), far_dev)
        send(frecv.at[0, :, pieces[p]], frecv.at[2, :, pieces[p]], fin, (p, 2), core_dev)
        put(frecv.at[0, :, pieces[p]], q_far, p, 1)
        arrive(frecv.at[1, :, pieces[p]], fin, (p, 1), core_dev)
        put(frecv.at[1, :, pieces[p]], q_core, p, 2)

    def last(p):
        arrive(frecv.at[2, :, pieces[p]], fin, (p, 2), core_dev)
        put(frecv.at[2, :, pieces[p]], q_diag, p, 3)

    first_terms(0, 0)
    spans = [pl.ds(lo * 256, (hi - lo) * 256) for lo, hi in halves]
    for n, span in enumerate(spans):
        back(q_diag, tp, into(gdiag), *halves[n])
        send(gdiag.at[:, span], rdiag.at[:, span], gx, (4 + n,), core_dev)
    first_terms(0, 1)
    for n, span in enumerate(spans):
        back(q_far, tp, into(acc), *halves[n])
        arrive(rdiag.at[:, span], gx, (4 + n,), core_dev)
        gfar[:, span] = (acc[:, span] + rdiag[:, span].astype(F32)).astype(BF16)
        send(gfar.at[:, span], rfar.at[:, span], gx, (n,), far_dev)
    first_terms(0, 2)
    first_terms(0, 3)
    own_term(0, 0)
    for st in range(4):
        first_terms(1, st)
    for st in range(1, 4):
        own_term(0, st)
    reduce_inner(0, 0)
    arrive(gh.at[chip_rows(2 - chip), pl.ds(tp, NEAR)], gx, (3,), far_dev)
    for st in range(4):
        first_terms(2, st)
    reduce_inner(0, 1)
    for st in range(4):
        own_term(1, st)
    reduce_inner(0, 2)
    for st in range(4):
        own_term(2, st)
    reduce_inner(0, 3)
    back(q_core, wide, into(gcore))
    send(gcore, rcore, gx, (2,), core_dev)
    for j in range(1, fi):
        arrive(ls.at[o, so, lax.rem(i + fi - j, fi)], ls2, (j,), inner_dev(j))
    for m, k in outer:
        mine = ls.at[o, so]
        send(mine, mine, ls3, (m, k), outer_dev(k, m))
    back(q, wide, into(acc))
    reduce_inner(1, 0)
    reduce_inner(1, 1)
    finish(0)
    reduce_inner(1, 2)
    reduce_inner(1, 3)
    arrive(rcore, gx, (2,), core_dev)
    acc[...] = acc[...] + rcore[...].astype(F32)
    reduce_inner(2, 0)
    reduce_inner(2, 1)
    reduce_inner(2, 2)
    finish(1)
    reduce_inner(2, 3)
    gfin = ctx.at[q]
    for n, span in enumerate(spans):
        arrive(rfar.at[:, span], gx, (n,), far_dev)
        gfin[:, span] = (acc[:, span] + rfar[:, span].astype(F32)).astype(BF16)
    out_ctx = local(gfin, gctx_out, 1)
    finish(2)
    for m, k in outer:
        there = ls.at[lax.rem(o + FO - k, FO), lax.rem(so + so_ways - m, so_ways)]
        arrive(there, ls3, (m, k), outer_dev(k, m))
    loss_out[...] = jnp.sum(ls[...], axis=(0, 1, 2))[0:1, 0:1] / count1
    for p in range(3):
        relay(p)
        last(p)
    out_ctx.wait()
    for copy in outs:
        copy.wait()
    for copy in sent:
        copy.wait_send()

    @pl.when(mid == 1)
    def _():
        for onward in zsent:
            hop(*onward).wait_send()


def hand_over(gctx_in, gw_in, gctx_out, gw_out, gctx, gw, gw32, sems):
    def parts_of(ref):
        step = ref.shape[1] // CHUNKS
        return [(slice(None), pl.ds(n * step, step)) for n in range(CHUNKS)]

    def copies(src, dst, kind):
        return [
            pltpu.make_async_copy(src.at[at], dst.at[at], sems.at[kind, n])
            for n, at in enumerate(parts_of(src))
        ]

    gw_loads = copies(gw_in, gw, 0)
    gctx_loads = copies(gctx_in, gctx, 1)
    gw_stores = copies(gw32, gw_out, 2)
    gctx_stores = copies(gctx, gctx_out, 3)
    for one, two in zip(gw_loads, gctx_loads):
        one.start()
        two.start()
    for n, at in enumerate(parts_of(gw)):
        gw_loads[n].wait()
        gw32[at] = gw[at].astype(F32)
        gw_stores[n].start()
        gctx_loads[n].wait()
        gctx_stores[n].start()
    for copy in gw_stores + gctx_stores:
        copy.wait()


def body(
    context,
    residual,
    target_rows,
    log_norm,
    norm_gain,
    out_proj,
    old_logprob,
    lengths,
    rewards,
    prompt_ids,
    placement,
):
    nrows, lmax, aw = context.shape
    dw = residual.shape[2]
    fsdp_ways = lax.axis_size("fsdp")
    seq_ways = lax.axis_size("seq")
    fi = fsdp_ways // FO
    so_ways = seq_ways // Q
    tokens = nrows * lmax
    blk = aw // fsdp_ways
    cq = dw // Q
    wide = cq + NEAR

    vmem = pl.BlockSpec(memory_space=pltpu.VMEM)
    anywhere = pl.BlockSpec(memory_space=pl.ANY)
    dma = pltpu.SemaphoreType.DMA
    buf = pltpu.VMEM
    gctx, gw, loss = pl.pallas_call(
        functools.partial(kernel, (fsdp_ways, seq_ways, nrows, lmax, dw, aw)),
        out_shape=(
            jax.ShapeDtypeStruct((tokens, aw), BF16),
            jax.ShapeDtypeStruct((blk, dw), BF16),
            jax.ShapeDtypeStruct((1, 1), F32),
        ),
        in_specs=[anywhere] * 11,
        out_specs=(anywhere, anywhere, vmem),
        scratch_shapes=[
            buf((aw, wide), BF16),
            buf((Q, tokens, aw), BF16),
            buf((aw, Q * tokens), BF16),
            buf((Q, tokens, wide), BF16),
            buf((Q, tokens, wide), BF16),
            buf((Q, tokens, wide), F32),
            buf((Q * tokens, wide), BF16),
            buf((Q, 8, Q * tokens), F32),
            buf((8, Q * tokens), F32),
            buf((FO, fi - 1, blk, cq), BF16),
            buf((FO, fi - 1, blk, cq), BF16),
            buf((FO, blk, cq), F32),
            buf((3, blk, cq), BF16),
            buf((4, blk, cq), BF16),
            buf((so_ways, blk, cq), BF16),
            buf((blk, cq), BF16),
            buf((3, blk, cq), BF16),
            buf((tokens, aw), F32),
            buf((tokens, aw), BF16),
            buf((tokens, aw), BF16),
            buf((tokens, aw), BF16),
            buf((tokens, aw), BF16),
            buf((tokens, aw), BF16),
            buf((tokens, aw), BF16),
            buf((FO, so_ways, fi, Q, 16, 128), F32),
            buf((FO, so_ways, fi, 8, 128), F32),
            buf((1, dw), F32),
            buf((1, wide), F32),
            buf((nrows, lmax), F32),
            buf((dw,), F32),
            buf((nrows, lmax), F32),
            buf((1, nrows), F32),
            buf((1, nrows), jnp.int32),
            buf((1, nrows), jnp.int32),
            buf((1, nrows), jnp.int32),
            dma((17,)),
            dma((2, 6, 2)),
            dma((2, 4, 2, fi)),
            dma((2, 11)),
            dma((2, 6)),
            dma((2, Q)),
            dma((2, 3, FO, fi)),
            dma((2, 3, FO)),
            dma((2, 3, so_ways)),
            dma((2, 3, 3)),
            dma((2, Q)),
            dma((2, fi)),
            dma((2, so_ways, FO)),
            dma((2, fi)),
            dma((2, so_ways, FO)),
        ],
        compiler_params=pltpu.CompilerParams(
            collective_id=0, has_side_effects=True, vmem_limit_bytes=62 << 20
        ),
        cost_estimate=pl.CostEstimate(
            flops=6 * tokens * aw * dw, bytes_accessed=12 * tokens * dw, transcendentals=tokens
        ),
    )(
        context.reshape(tokens, aw),
        residual.reshape(tokens, dw),
        target_rows.reshape(tokens, dw),
        log_norm,
        norm_gain,
        out_proj,
        old_logprob,
        rewards.reshape(1, nrows),
        prompt_ids.reshape(1, nrows),
        lengths.reshape(1, nrows),
        placement.reshape(1, nrows),
    )
    gctx, gw = pl.pallas_call(
        hand_over,
        out_shape=(
            jax.ShapeDtypeStruct((tokens, aw), BF16),
            jax.ShapeDtypeStruct((blk, dw), F32),
        ),
        in_specs=[anywhere] * 2,
        out_specs=(anywhere,) * 2,
        scratch_shapes=[
            buf((tokens, aw), BF16),
            buf((blk, dw), BF16),
            buf((blk, dw), F32),
            dma((4, CHUNKS)),
        ],
        compiler_params=pltpu.CompilerParams(vmem_limit_bytes=VM2 << 20),
        cost_estimate=pl.CostEstimate(
            flops=blk * dw, bytes_accessed=4 * tokens * aw + 6 * blk * dw, transcendentals=0
        ),
    )(gctx, gw)
    return (gctx.reshape(nrows, lmax, aw), gw, loss.reshape(()))


def solution(mesh):
    return jax.shard_map(
        body,
        mesh=mesh,
        in_specs=(
            P("fsdp", "seq", None),
            P("fsdp", "seq", None),
            P("fsdp", "seq", None),
            P("fsdp", "seq"),
            P(),
            P("fsdp", None),
            P("fsdp", "seq"),
            P("fsdp", "seq"),
            P("fsdp", "seq"),
            P("fsdp", "seq"),
            P("fsdp", "seq"),
        ),
        out_specs=(P("fsdp", "seq", None), P("fsdp", None), P()),
        check_vma=False,
    )
```

```python
import functools
import math

import jax
import jax.numpy as jnp
from jax import lax
from jax.experimental import pallas as pl
from jax.experimental.pallas import tpu as pltpu
from jax.sharding import PartitionSpec as P

GS = 16
FO = 4
Q = 4
NEAR = 128
CHUNKS = 4
VM2 = 62
MESH = pl.DeviceIdType.MESH
F32 = jnp.float32
BF16 = jnp.bfloat16
NT = (((1,), (1,)), ((), ()))


def kernel(
    dims,
    ctx_in,
    res_in,
    tgt_in,
    lognorm_in,
    gain_in,
    w_in,
    old_in,
    rewards_in,
    prompt_ids_in,
    lengths_in,
    placement_in,
    gctx_out,
    gw_out,
    loss_out,
    w,
    ctx,
    ctxt,
    res,
    tgt,
    hid,
    gh,
    sm,
    rb,
    dws,
    irecv,
    part,
    obuf,
    zr,
    mrecv,
    fsend,
    frecv,
    acc,
    gdiag,
    gcore,
    gfar,
    rdiag,
    rcore,
    rfar,
    pk,
    ls,
    gain,
    gain2,
    lognorm,
    gain1,
    old,
    rewards,
    prompt_ids,
    lengths,
    placement,
    loc,
    ag_z,
    ag_i,
    tok,
    gx,
    sx,
    rs_i,
    rs_z,
    rs_m,
    fin,
    pk1,
    pk2,
    pk3,
    ls2,
    ls3,
):
    fsdp_ways, seq_ways, nrows, lmax, dw, aw = dims
    fi = fsdp_ways // FO
    so_ways = seq_ways // Q
    tokens = nrows * lmax
    blk = aw // fsdp_ways
    cq = dw // Q
    prompts = nrows * fsdp_ways * seq_ways // GS
    prows = max(8, prompts)
    all_tokens = tokens * fsdp_ways * seq_ways
    f = lax.axis_index("fsdp")
    s = lax.axis_index("seq")
    o = f // fi
    i = lax.rem(f, fi)
    so = s // Q
    q = lax.rem(s, Q)
    c = lax.rem(q, 2)

    def outer_dev(k, m=0):
        return (lax.rem(o + k, FO) * fi + i, lax.rem(so + m, so_ways) * Q + q)

    def inner_dev(j):
        return (o * fi + lax.rem(i + j, fi), s)

    def group_dev(k):
        return (f, so * Q + lax.rem(q + k, Q))

    q_core = q + 1 - 2 * c
    q_far = lax.rem(q + 2, Q)
    q_diag = lax.rem(q_core + 2, Q)
    core_dev = (f, so * Q + q_core)
    far_dev = (f, so * Q + q_far)
    diag_dev = (f, so * Q + q_diag)
    chip = q - c
    wide = cq + NEAR
    tp = cq - NEAR
    oh = o // 2
    mid = lax.rem(lax.rem(o, 2) + oh, 2)
    partner = o + 1 - 2 * lax.rem(o, 2)
    far_mid = 2 - oh
    far_end = 3 - 3 * oh
    outer = [(m, k) for k in range(FO) for m in range(so_ways) if (m, k) != (0, 0)]

    def rows_of(owner):
        return pl.ds(pl.multiple_of(owner * blk, blk), blk)

    def cols_of(quarter):
        return pl.ds(pl.multiple_of(quarter * cq, 128), cq)

    def at_outer(d):
        return (d * fi + i, s)

    def tp_of(quarter):
        return pl.ds(pl.multiple_of(quarter * cq, 128), tp)

    def near_of(quarter):
        return pl.ds(pl.multiple_of(quarter * cq + tp, 128), NEAR)

    def toks_of(quarter):
        return pl.ds(pl.multiple_of(quarter * tokens, 128), tokens)

    def local(src, dst, index):
        copy = pltpu.make_async_copy(src, dst, loc.at[index])
        copy.start()
        return copy

    barrier = pltpu.get_barrier_semaphore()
    peers = [outer_dev(k, m) for m, k in outer] if so_ways > 1 else [at_outer(partner)]
    peers += [inner_dev(j) for j in range(1, fi)]
    peers += [group_dev(k) for k in range(1, Q)]
    for peer in peers:
        pl.semaphore_signal(barrier, inc=1, device_id=peer, device_id_type=MESH)
    if so_ways == 1:

        @pl.when(mid == 1)
        def _():
            pl.semaphore_signal(
                barrier, inc=1, device_id=at_outer(far_mid), device_id_type=MESH
            )


    small = [
        local(src, dst, 7 + n)
        for n, (src, dst) in enumerate(
            (
                (old_in, old),
                (rewards_in, rewards),
                (prompt_ids_in, prompt_ids),
                (lengths_in, lengths),
                (placement_in, placement),
                (lognorm_in, lognorm),
                (gain_in, gain1),
            )
        )
    ]
    here, beyond = pl.ds(0, cq), pl.ds(cq, NEAR)
    own_w = [
        local(w_in.at[:, cols_of(q)], w.at[rows_of(f), here], 0),
        local(w_in.at[:, near_of(q_far)], w.at[rows_of(f), beyond], 1),
    ]
    own_ctx = local(ctx_in, ctx.at[q], 2)
    own_rows = [
        local(res_in.at[:, cols_of(q)], res.at[q, :, here], 3),
        local(res_in.at[:, near_of(q_far)], res.at[q, :, beyond], 4),
        local(tgt_in.at[:, cols_of(q)], tgt.at[q, :, here], 5),
        local(tgt_in.at[:, near_of(q_far)], tgt.at[q, :, beyond], 6),
    ]

    for copy in small:
        copy.wait()
    at_home = (o, so, i, q)
    pk[at_home] = jnp.zeros((16, 128), F32)
    pk[at_home + (pl.ds(0, nrows), slice(None))] = old[...]
    for n, field in enumerate((rewards, prompt_ids, lengths, placement)):
        for r in range(nrows):
            pk[at_home + (pl.ds((n + 1) * nrows + r, 1), slice(None))] = jnp.broadcast_to(
                field[:, r : r + 1].astype(F32), (1, 128)
            )
    pk[at_home + (pl.ds(5 * nrows, nrows), slice(None))] = lognorm[...]
    gain[...] = gain1[...].reshape(1, dw)
    gain2[:, 0:cq] = gain[:, cols_of(q)]
    gain2[:, cq:wide] = gain[:, near_of(q_far)]

    pl.semaphore_wait(barrier, len(peers) + (mid if so_ways == 1 else 0))

    sent = []

    def send(src, dst, sems, index, dev):
        copy = pltpu.make_async_remote_copy(
            src_ref=src,
            dst_ref=dst,
            send_sem=sems.at[(0,) + index],
            recv_sem=sems.at[(1,) + index],
            device_id=dev,
            device_id_type=MESH,
        )
        copy.start()
        sent.append(copy)

    def arrive(dst, sems, index, dev):
        pltpu.make_async_remote_copy(
            src_ref=dst,
            dst_ref=dst,
            send_sem=sems.at[(0,) + index],
            recv_sem=sems.at[(1,) + index],
            device_id=dev,
            device_id_type=MESH,
        ).wait_recv()

    cut = (blk // 2 + 15) // 16 * 16
    row_halves = ((0, cut), (cut, blk - cut))

    def block(owner, h):
        first, count = row_halves[h]
        return w.at[pl.ds(pl.multiple_of(owner * blk + first, 16), count), :]

    for k in range(1, Q):
        mine = pk.at[o, so, i, q]
        send(mine, mine, pk1, (k,), group_dev(k))
    for copy in own_w:
        copy.wait()
    for h in range(2):
        for j in range(1, fi):
            send(block(f, h), block(f, h), ag_i, (3, h, j), inner_dev(j))

    def hop(src, n, h, goal):
        return pltpu.make_async_remote_copy(
            src_ref=src,
            dst_ref=src,
            send_sem=ag_z.at[0, n, h],
            recv_sem=ag_z.at[1, n % 3, h],
            device_id=at_outer(goal),
            device_id_type=MESH,
        )

    zsent = [(block(f, h), 4, h, far_mid) for h in range(2)]

    @pl.when(mid == 1)
    def _():
        for onward in zsent[:2]:
            hop(*onward).start()

    for h in range(2):
        send(block(f, h), block(f, h), ag_z, (0, h), at_outer(partner))
    send(ctx_in, ctx.at[q], tok, (0,), far_dev)
    send(ctx_in, ctx.at[q], tok, (1,), core_dev)
    for n, (src, dst) in enumerate(((res_in, res), (tgt_in, tgt))):
        send(src.at[:, cols_of(q_core)], dst.at[q, :, here], tok, (3 + n,), core_dev)
        send(src.at[:, near_of(q_diag)], dst.at[q, :, beyond], tok, (5 + n,), core_dev)
    over = pl.ds(0, tp)
    for n, (quarter, dev) in enumerate(((q_far, far_dev), (q_diag, diag_dev))):
        send(res_in.at[:, tp_of(quarter)], res.at[q, :, over], tok, (7 + 2 * n,), dev)
        send(tgt_in.at[:, tp_of(quarter)], tgt.at[q, :, over], tok, (8 + 2 * n,), dev)

    def turn(a):
        @pl.loop(0, aw // 256)
        def _(t):
            span = pl.ds(pl.multiple_of(t * 256, 256), 256)
            ctxt[span, toks_of(a)] = ctx[a, :, span].T

    for k in range(1, Q):
        there = pk.at[o, so, i, lax.rem(q + Q - k, Q)]
        arrive(there, pk1, (k,), group_dev(k))
    for j in range(1, fi):
        mine = pk.at[o, so, i]
        send(mine, mine, pk2, (j,), inner_dev(j))
    own_ctx.wait()
    turn(q)
    for j in range(1, fi):
        there = pk.at[o, so, lax.rem(i + fi - j, fi)]
        arrive(there, pk2, (j,), inner_dev(j))

    def pass_half(n, h, source, goal):
        got = block(source * fi + i, h)
        arrive(got, ag_z, (n, h), at_outer(partner))
        onward = (got, 5 if n == 0 else n, h, goal)
        zsent.append(onward)

        @pl.when(mid == 1)
        def _():
            hop(*onward).start()

        for j in range(1, fi):
            send(got, got, ag_i, (n, h, j), inner_dev(j))

    def pass_on(n, source, goal):
        for h in range(2):
            pass_half(n, h, source, goal)

    pass_on(0, partner, far_mid)
    arrive(ctx.at[q_core], tok, (1,), core_dev)
    turn(q_core)
    pass_on(1, far_mid, partner)
    pass_on(2, far_end, partner)
    for m, k in outer:
        mine = pk.at[o, so]
        send(mine, mine, pk3, (m, k), outer_dev(k, m))
    arrive(ctx.at[q_far], tok, (0,), far_dev)
    send(ctx.at[q_far], ctx.at[q_far], tok, (2,), core_dev)
    turn(q_far)
    arrive(ctx.at[q_diag], tok, (2,), core_dev)
    turn(q_diag)

    def gathered(n, source):
        for j in range(1, fi):
            owner = source * fi + lax.rem(i + fi - j, fi)
            for h in range(2):
                arrive(block(owner, h), ag_i, (n, h, j), inner_dev(j))

    def forward(first, depth, fresh):
        span = pl.ds(pl.multiple_of(first * fi * blk, 128), depth * fi * blk)

        def add(a, width):
            h = jnp.dot(ctx[a, :, span], w[span, 0:width], preferred_element_type=F32)
            hid[a, :, 0:width] = h if fresh else hid[a, :, 0:width] + h

        @pl.loop(0, 2)
        def _(t):
            add(chip + t, wide)

        @pl.loop(0, 2)
        def _(t):
            add(2 - chip + t, tp)

    gathered(3, o)
    gathered(0, partner)
    forward(2 * oh, 2, True)
    for m, k in outer:
        there = pk.at[lax.rem(o + FO - k, FO), lax.rem(so + so_ways - m, so_ways)]
        arrive(there, pk3, (m, k), outer_dev(k, m))

    prompt_row = lax.broadcasted_iota(jnp.int32, (prows, 128), 0).astype(F32)
    zero_p = jnp.zeros((prows, 128), F32)
    zero_r = jnp.zeros((1, 128), F32)

    def over_devices(fa, carry):
        for sa in range(seq_ways):
            at = (fa // fi, sa // Q, lax.rem(fa, fi), sa % Q)
            for r in range(nrows):
                gsum, gsq, count = carry
                reward = pk[at + (pl.ds(nrows + r, 1), slice(None))]
                prompt = pk[at + (pl.ds(2 * nrows + r, 1), slice(None))]
                length = pk[at + (pl.ds(3 * nrows + r, 1), slice(None))]
                hot = prompt == prompt_row
                gsum = gsum + jnp.where(hot, reward, 0.0)
                gsq = gsq + jnp.where(hot, reward * reward, 0.0)
                carry = (gsum, gsq, count + length)
        return carry

    gsum, gsq, count = lax.fori_loop(0, fsdp_ways, over_devices, (zero_p, zero_p, zero_r))
    gmean = gsum / GS
    gvar = gsq / GS - gmean * gmean
    offset = lax.broadcasted_iota(jnp.int32, (1, lmax), 1).astype(F32)
    count1 = count[:, 0:1]

    for a in range(Q):

        def over_column(fa, carry, a=a):
            at = (fa // fi, so, lax.rem(fa, fi), a)
            for r in range(nrows):
                past = pk[at + (pl.ds(r, 1), slice(None))]
                reward = pk[at + (pl.ds(nrows + r, 1), slice(None))]
                prompt = pk[at + (pl.ds(2 * nrows + r, 1), slice(None))]
                length = pk[at + (pl.ds(3 * nrows + r, 1), slice(None))]
                dest = pk[at + (pl.ds(4 * nrows + r, 1), slice(None))]
                hot = prompt == prompt_row
                mean = jnp.sum(jnp.where(hot, gmean, 0.0), axis=0, keepdims=True)
                var = jnp.sum(jnp.where(hot, gvar, 0.0), axis=0, keepdims=True)
                adv = (reward - mean) / jnp.sqrt(var + 0.25)
                fresh = []
                for j in range(nrows):
                    chosen = dest == (f * nrows + j).astype(F32)
                    l_old, l_adv, l_len = carry[3 * j : 3 * j + 3]
                    fresh += [
                        l_old + jnp.where(chosen, past, 0.0),
                        l_adv + jnp.where(chosen, adv, 0.0),
                        l_len + jnp.where(chosen, length, 0.0),
                    ]
                carry = tuple(fresh)
            return carry

        learned = lax.fori_loop(0, fsdp_ways, over_column, (zero_r,) * (3 * nrows))
        for j in range(nrows):
            l_old, l_adv, l_len = learned[3 * j : 3 * j + 3]
            at = pl.ds(a * tokens + j * lmax, lmax)
            norm = pk[o, so, i, a, pl.ds(5 * nrows + j, 1), :]
            rb[0:1, at] = norm + l_old
            rb[1:2, at] = l_adv
            rb[2:3, at] = (offset < l_len).astype(F32)

    gathered(1, far_mid)
    forward(far_mid, 1, False)
    gathered(2, far_end)
    forward(far_end, 1, False)

    lane = lax.broadcasted_iota(jnp.int32, (tokens, 128), 1)

    def sums(a, width):
        h = hid[a, :, 0:width] + res[a, :, 0:width].astype(F32)
        hid[a, :, 0:width] = h
        v = gain2[:, 0:width] * tgt[a, :, 0:width].astype(F32)
        ssq = jnp.sum(h * h, axis=1, keepdims=True)
        shv = jnp.sum(h * v, axis=1, keepdims=True)
        both = jnp.where(lane == 0, ssq, jnp.where(lane == 1, shv, 0.0))
        sm[q, :, toks_of(a)] = both.T[0:8, :]

    for copy in own_rows:
        copy.wait()
    sums(q, wide)
    for n, ref in enumerate((res, tgt)):
        arrive(ref.at[q_core, :, here], tok, (3 + n,), core_dev)
        arrive(ref.at[q_core, :, beyond], tok, (5 + n,), core_dev)
    sums(q_core, wide)
    for n, (quarter, dev) in enumerate(((q_far, far_dev), (q_diag, diag_dev))):
        arrive(res.at[quarter, :, over], tok, (7 + 2 * n,), dev)
        arrive(tgt.at[quarter, :, over], tok, (8 + 2 * n,), dev)
        sums(quarter, tp)
    for k in range(1, Q):
        send(sm.at[q], sm.at[q], sx, (k,), group_dev(k))
    for k in range(1, Q):
        arrive(sm.at[lax.rem(q + Q - k, Q)], sx, (k,), group_dev(k))
    ssq = sm[0, 0:1, :] + sm[1, 0:1, :] + sm[2, 0:1, :] + sm[3, 0:1, :]
    shv = sm[0, 1:2, :] + sm[1, 1:2, :] + sm[2, 1:2, :] + sm[3, 1:2, :]
    token_adv = rb[1:2, :]
    valid = rb[2:3, :]
    rinv = lax.rsqrt(ssq / dw + 1e-06)
    score = shv * rinv
    ratio = jnp.exp(score - rb[0:1, :])
    plain = ratio * token_adv
    clipped = jnp.clip(ratio, 0.8, 1.2) * token_adv
    loss_local = jnp.sum(valid * -jnp.minimum(plain, clipped), axis=1, keepdims=True)
    dscore = -valid * jnp.where(plain <= clipped, plain, 0.0) / count1
    rb[3:4, :] = dscore * rinv * (32.0 * all_tokens * math.sqrt(dw))
    rb[4:5, :] = rinv * rinv * shv / dw

    row = lax.broadcasted_iota(jnp.int32, (128, tokens), 0)

    def make_gh(a, width):
        both = jnp.where(row == 0, rb[3:4, toks_of(a)], rb[4:5, toks_of(a)]).T
        lead = both[:, 0:1]
        inner_scale = both[:, 1:2]
        v = gain2[:, 0:width] * tgt[a, :, 0:width].astype(F32)
        gh[toks_of(a), 0:width] = (lead * (v - hid[a, :, 0:width] * inner_scale)).astype(BF16)

    @pl.loop(0, 2)
    def _(t):
        make_gh(chip + t, wide)

    def chip_rows(first):
        return pl.ds(pl.multiple_of(first * tokens, 128), 2 * tokens)

    send(
        gh.at[chip_rows(chip), beyond],
        gh.at[chip_rows(chip), pl.ds(tp, NEAR)],
        gx,
        (3,),
        far_dev,
    )

    @pl.loop(0, 2)
    def _(t):
        make_gh(2 - chip + t, tp)

    ls[o, so, i] = jnp.broadcast_to(loss_local, (8, 128))
    for j in range(1, fi):
        mine = ls.at[o, so, i]
        send(mine, mine, ls2, (j,), inner_dev(j))

    starts = ((0, 256), (256, 256), (512, cq - 512))
    pieces = [pl.ds(lo, width) for lo, width in starts]

    def term(owner, p):
        return jnp.dot(ctxt[rows_of(owner), :], gh[:, pieces[p]], preferred_element_type=F32)

    steps = aw // 256
    halves = ((0, steps // 2), (steps // 2, steps))

    def back(a, width, store, lo=0, hi=steps):
        @pl.loop(lo, hi)
        def _(t):
            span = pl.ds(pl.multiple_of(t * 256, 256), 256)
            store(
                span,
                lax.dot_general(
                    gh[toks_of(a), 0:width], w[span, 0:width], NT, preferred_element_type=F32
                ),
            )

    def into(ref):
        def store(span, value):
            ref[:, span] = value.astype(ref.dtype)

        return store

    dests = (far_end, far_mid, partner, o)

    def first_terms(p, st):
        for j in range(1, fi):
            owner = dests[st] * fi + lax.rem(i + j, fi)
            dws[st, j - 1, :, pieces[p]] = term(owner, p).astype(BF16)
            send(
                dws.at[st, j - 1, :, pieces[p]],
                irecv.at[st, j - 1, :, pieces[p]],
                rs_i,
                (p, st, j),
                inner_dev(j),
            )

    def own_term(p, st):
        part[st, :, pieces[p]] = term(dests[st] * fi + i, p)

    def zin(p, n):
        return zr.at[n, :, pieces[p]]

    def reduce_inner(p, st):
        for j in range(1, fi):
            arrive(irecv.at[st, j - 1, :, pieces[p]], rs_i, (p, st, j), inner_dev(j))
        total = part[st, :, pieces[p]]
        for j in range(1, fi):
            total = total + irecv[st, j - 1, :, pieces[p]].astype(F32)
        if st == 3:
            part[3, :, pieces[p]] = total
            return
        obuf[st, :, pieces[p]] = total.astype(BF16)
        slot, goal = st, partner
        if st < 2:

            @pl.when(mid == 1)
            def _():
                arrive(zin(p, st), rs_z, (p, st), at_outer(partner))
                both = part[st, :, pieces[p]]
                for j in range(1, fi):
                    both = both + irecv[st, j - 1, :, pieces[p]].astype(F32)
                obuf[st, :, pieces[p]] = (both + zr[st, :, pieces[p]].astype(F32)).astype(BF16)

            slot = mid * 3 + (1 - mid) * st
            goal = mid * dests[st] + (1 - mid) * partner
        copy = pltpu.make_async_remote_copy(
            src_ref=obuf.at[st, :, pieces[p]],
            dst_ref=zr.at[slot, :, pieces[p]],
            send_sem=rs_z.at[0, p, st],
            recv_sem=rs_z.at[1, p, slot],
            device_id=at_outer(goal),
            device_id_type=MESH,
        )
        copy.start()
        sent.append(copy)

    scale = 1.0 / math.sqrt(all_tokens)
    outs = []

    def put(ref, quarter, p, n):
        lo, width = starts[p]
        at = pl.ds(pl.multiple_of(quarter * cq + lo, 128), width)
        outs.append(local(ref, gw_out.at[:, at], 5 + 4 * p + n))

    def finish(p):
        for n in (2, 3):
            arrive(zin(p, n), rs_z, (p, n), at_outer(partner))
        total = part[3, :, pieces[p]]
        for n in (2, 3):
            total = total + zr[n, :, pieces[p]].astype(F32)
        if so_ways > 1:
            mrecv[so, :, pieces[p]] = total.astype(BF16)
            for m in range(1, so_ways):
                mine = mrecv.at[so, :, pieces[p]]
                send(mine, mine, rs_m, (p, m), outer_dev(0, m))
            for m in range(1, so_ways):
                there = mrecv.at[lax.rem(so + so_ways - m, so_ways), :, pieces[p]]
                arrive(there, rs_m, (p, m), outer_dev(0, m))
            total = mrecv[0, :, pieces[p]].astype(F32)
            for m in range(1, so_ways):
                total = total + mrecv[m, :, pieces[p]].astype(F32)
        fsend[:, pieces[p]] = (total * scale).astype(BF16)
        for n, dev in ((0, far_dev), (1, core_dev)):
            send(fsend.at[:, pieces[p]], frecv.at[n, :, pieces[p]], fin, (p, n), dev)
        put(fsend.at[:, pieces[p]], q, p, 0)

    def relay(p):
        arrive(frecv.at[0, :, pieces[p]], fin, (p, 0), far_dev)
        send(frecv.at[0, :, pieces[p]], frecv.at[2, :, pieces[p]], fin, (p, 2), core_dev)
        put(frecv.at[0, :, pieces[p]], q_far, p, 1)
        arrive(frecv.at[1, :, pieces[p]], fin, (p, 1), core_dev)
        put(frecv.at[1, :, pieces[p]], q_core, p, 2)

    def last(p):
        arrive(frecv.at[2, :, pieces[p]], fin, (p, 2), core_dev)
        put(frecv.at[2, :, pieces[p]], q_diag, p, 3)

    for st in range(4):
        first_terms(0, st)
    spans = [pl.ds(lo * 256, (hi - lo) * 256) for lo, hi in halves]
    for n, span in enumerate(spans):
        back(q_diag, tp, into(gdiag), *halves[n])
        send(gdiag.at[:, span], rdiag.at[:, span], gx, (4 + n,), core_dev)
    own_term(0, 0)
    for n, span in enumerate(spans):
        back(q_far, tp, into(acc), *halves[n])
        arrive(rdiag.at[:, span], gx, (4 + n,), core_dev)
        gfar[:, span] = (acc[:, span] + rdiag[:, span].astype(F32)).astype(BF16)
        send(gfar.at[:, span], rfar.at[:, span], gx, (n,), far_dev)
    for st in range(4):
        first_terms(1, st)
    for st in range(1, 4):
        own_term(0, st)
    reduce_inner(0, 0)
    arrive(gh.at[chip_rows(2 - chip), pl.ds(tp, NEAR)], gx, (3,), far_dev)
    for st in range(4):
        first_terms(2, st)
    reduce_inner(0, 1)
    for st in range(4):
        own_term(1, st)
    reduce_inner(0, 2)
    for st in range(4):
        own_term(2, st)
    reduce_inner(0, 3)
    back(q_core, wide, into(gcore))
    send(gcore, rcore, gx, (2,), core_dev)
    for j in range(1, fi):
        arrive(ls.at[o, so, lax.rem(i + fi - j, fi)], ls2, (j,), inner_dev(j))
    for m, k in outer:
        mine = ls.at[o, so]
        send(mine, mine, ls3, (m, k), outer_dev(k, m))
    back(q, wide, into(acc))
    reduce_inner(1, 0)
    reduce_inner(1, 1)
    finish(0)
    reduce_inner(1, 2)
    reduce_inner(1, 3)
    arrive(rcore, gx, (2,), core_dev)
    acc[...] = acc[...] + rcore[...].astype(F32)
    reduce_inner(2, 0)
    reduce_inner(2, 1)
    reduce_inner(2, 2)
    finish(1)
    reduce_inner(2, 3)
    gfin = ctx.at[q]
    for n, span in enumerate(spans):
        arrive(rfar.at[:, span], gx, (n,), far_dev)
        gfin[:, span] = (acc[:, span] + rfar[:, span].astype(F32)).astype(BF16)
    out_ctx = local(gfin, gctx_out, 1)
    finish(2)
    for m, k in outer:
        there = ls.at[lax.rem(o + FO - k, FO), lax.rem(so + so_ways - m, so_ways)]
        arrive(there, ls3, (m, k), outer_dev(k, m))
    loss_out[...] = jnp.sum(ls[...], axis=(0, 1, 2))[0:1, 0:1] / count1
    for p in range(3):
        relay(p)
        last(p)
    out_ctx.wait()
    for copy in outs:
        copy.wait()
    for copy in sent:
        copy.wait_send()

    @pl.when(mid == 1)
    def _():
        for onward in zsent:
            hop(*onward).wait_send()


def hand_over(gctx_in, gw_in, gctx_out, gw_out, gctx, gw, gw32, sems):
    def parts_of(ref):
        step = ref.shape[1] // CHUNKS
        return [(slice(None), pl.ds(n * step, step)) for n in range(CHUNKS)]

    def copies(src, dst, kind):
        return [
            pltpu.make_async_copy(src.at[at], dst.at[at], sems.at[kind, n])
            for n, at in enumerate(parts_of(src))
        ]

    gw_loads = copies(gw_in, gw, 0)
    gctx_loads = copies(gctx_in, gctx, 1)
    gw_stores = copies(gw32, gw_out, 2)
    gctx_stores = copies(gctx, gctx_out, 3)
    for one, two in zip(gw_loads, gctx_loads):
        one.start()
        two.start()
    for n, at in enumerate(parts_of(gw)):
        gw_loads[n].wait()
        gw32[at] = gw[at].astype(F32)
        gw_stores[n].start()
        gctx_loads[n].wait()
        gctx_stores[n].start()
    for copy in gw_stores + gctx_stores:
        copy.wait()


def body(
    context,
    residual,
    target_rows,
    log_norm,
    norm_gain,
    out_proj,
    old_logprob,
    lengths,
    rewards,
    prompt_ids,
    placement,
):
    nrows, lmax, aw = context.shape
    dw = residual.shape[2]
    fsdp_ways = lax.axis_size("fsdp")
    seq_ways = lax.axis_size("seq")
    fi = fsdp_ways // FO
    so_ways = seq_ways // Q
    tokens = nrows * lmax
    blk = aw // fsdp_ways
    cq = dw // Q
    wide = cq + NEAR

    vmem = pl.BlockSpec(memory_space=pltpu.VMEM)
    anywhere = pl.BlockSpec(memory_space=pl.ANY)
    dma = pltpu.SemaphoreType.DMA
    buf = pltpu.VMEM
    gctx, gw, loss = pl.pallas_call(
        functools.partial(kernel, (fsdp_ways, seq_ways, nrows, lmax, dw, aw)),
        out_shape=(
            jax.ShapeDtypeStruct((tokens, aw), BF16),
            jax.ShapeDtypeStruct((blk, dw), BF16),
            jax.ShapeDtypeStruct((1, 1), F32),
        ),
        in_specs=[anywhere] * 11,
        out_specs=(anywhere, anywhere, vmem),
        scratch_shapes=[
            buf((aw, wide), BF16),
            buf((Q, tokens, aw), BF16),
            buf((aw, Q * tokens), BF16),
            buf((Q, tokens, wide), BF16),
            buf((Q, tokens, wide), BF16),
            buf((Q, tokens, wide), F32),
            buf((Q * tokens, wide), BF16),
            buf((Q, 8, Q * tokens), F32),
            buf((8, Q * tokens), F32),
            buf((FO, fi - 1, blk, cq), BF16),
            buf((FO, fi - 1, blk, cq), BF16),
            buf((FO, blk, cq), F32),
            buf((3, blk, cq), BF16),
            buf((4, blk, cq), BF16),
            buf((so_ways, blk, cq), BF16),
            buf((blk, cq), BF16),
            buf((3, blk, cq), BF16),
            buf((tokens, aw), F32),
            buf((tokens, aw), BF16),
            buf((tokens, aw), BF16),
            buf((tokens, aw), BF16),
            buf((tokens, aw), BF16),
            buf((tokens, aw), BF16),
            buf((tokens, aw), BF16),
            buf((FO, so_ways, fi, Q, 16, 128), F32),
            buf((FO, so_ways, fi, 8, 128), F32),
            buf((1, dw), F32),
            buf((1, wide), F32),
            buf((nrows, lmax), F32),
            buf((dw,), F32),
            buf((nrows, lmax), F32),
            buf((1, nrows), F32),
            buf((1, nrows), jnp.int32),
            buf((1, nrows), jnp.int32),
            buf((1, nrows), jnp.int32),
            dma((17,)),
            dma((2, 6, 2)),
            dma((2, 4, 2, fi)),
            dma((2, 11)),
            dma((2, 6)),
            dma((2, Q)),
            dma((2, 3, FO, fi)),
            dma((2, 3, FO)),
            dma((2, 3, so_ways)),
            dma((2, 3, 3)),
            dma((2, Q)),
            dma((2, fi)),
            dma((2, so_ways, FO)),
            dma((2, fi)),
            dma((2, so_ways, FO)),
        ],
        compiler_params=pltpu.CompilerParams(
            collective_id=0, has_side_effects=True, vmem_limit_bytes=62 << 20
        ),
        cost_estimate=pl.CostEstimate(
            flops=6 * tokens * aw * dw, bytes_accessed=12 * tokens * dw, transcendentals=tokens
        ),
    )(
        context.reshape(tokens, aw),
        residual.reshape(tokens, dw),
        target_rows.reshape(tokens, dw),
        log_norm,
        norm_gain,
        out_proj,
        old_logprob,
        rewards.reshape(1, nrows),
        prompt_ids.reshape(1, nrows),
        lengths.reshape(1, nrows),
        placement.reshape(1, nrows),
    )
    gctx, gw = pl.pallas_call(
        hand_over,
        out_shape=(
            jax.ShapeDtypeStruct((tokens, aw), BF16),
            jax.ShapeDtypeStruct((blk, dw), F32),
        ),
        in_specs=[anywhere] * 2,
        out_specs=(anywhere,) * 2,
        scratch_shapes=[
            buf((tokens, aw), BF16),
            buf((blk, dw), BF16),
            buf((blk, dw), F32),
            dma((4, CHUNKS)),
        ],
        compiler_params=pltpu.CompilerParams(vmem_limit_bytes=VM2 << 20),
        cost_estimate=pl.CostEstimate(
            flops=blk * dw, bytes_accessed=4 * tokens * aw + 6 * blk * dw, transcendentals=0
        ),
    )(gctx, gw)
    return (gctx.reshape(nrows, lmax, aw), gw, loss.reshape(()))


def solution(mesh):
    return jax.shard_map(
        body,
        mesh=mesh,
        in_specs=(
            P("fsdp", "seq", None),
            P("fsdp", "seq", None),
            P("fsdp", "seq", None),
            P("fsdp", "seq"),
            P(),
            P("fsdp", None),
            P("fsdp", "seq"),
            P("fsdp", "seq"),
            P("fsdp", "seq"),
            P("fsdp", "seq"),
            P("fsdp", "seq"),
        ),
        out_specs=(P("fsdp", "seq", None), P("fsdp", None), P()),
        check_vma=False,
    )
```
